128 devices in a mesh: ctx: 32 (over z, x, core), tp: 4 (over y).
Axes of the slice: x: 4, y: 4, z: 4, core: 2. Of those that a mesh axis runs over, the one named last changes fastest.
Arguments:
- hidden_states: bfloat16 [3072, 8192], P('ctx', 'tp'), may hold values from -6 to 6
- counts: int32 [32], P('ctx'), may hold values from 24 to 72, as said below
- selected: int32 [32, 72], P('ctx'), may hold values from 0 to 95, as said below
- router_weight: float32 [3072], P('ctx'), may hold values from 0.25 to 1.5
- norm_gain: float32 [8192], P('tp'), may hold values from 0.25 to 1.75
- w_gate: bfloat16 [8192, 28672], P('tp', 'ctx'), may hold values from -0.0625 to 0.0625
- w_up: bfloat16 [8192, 28672], P('tp', 'ctx'), may hold values from -0.0625 to 0.0625
- w_down: bfloat16 [28672, 8192], P('ctx', 'tp'), may hold values from -0.03125 to 0.03125
Outputs:
- block_out: bfloat16 [3072, 8192], P('ctx', 'tp')
The draws below stay inside these ranges and needn't reach their ends.
Inputs may be any that keep to these rules, and one draw needn't show every extreme that they name: The counts sum to 1536; for every shard s the counts of the shards before s sum to between s * 48 - 48 // 4 and s * 48 + 48 // 4. `selected`: the entries of a row are distinct; only the first counts[s] entries of row s are used.
All inputs are finite; a program needn't handle non-finite values.
Results may differ from the reference program's by a relative error of at most 0.014.
Values may be sent and summed in bfloat16 or wider, within the bound.
A program may use at most 128 MiB of HBM per device.

```python
import jax
import jax.numpy as jnp
from jax import lax

D = 8192
FF = 28672
TOK_DEV = 96
SEL = 48
MAXSEL = 72
TOKENS = 3072
N_CTX = 32


def draw_counts(key, part):
    quarter = SEL // 4
    first_key = jax.random.fold_in(key, 11)
    second_key = jax.random.fold_in(key, 12)
    excess = jax.random.randint(first_key, (N_CTX,), -quarter, quarter + 1).astype(jnp.int32)
    positions = jnp.arange(N_CTX, dtype=jnp.int32)
    excess = jnp.where(positions == N_CTX - 1, 0, excess)
    heavy = jax.random.randint(second_key, (), 1, N_CTX - 1).astype(jnp.int32)
    excess = jnp.where(positions == heavy, quarter, excess)
    excess = jnp.where(positions == heavy - 1, -quarter, excess)
    before = jnp.concatenate([jnp.zeros((1,), jnp.int32), excess[:-1]])
    return (SEL + excess - before).astype(jnp.int32)


def draw_selected(key, part):
    subkeys = jax.random.split(jax.random.fold_in(key, 21), N_CTX)
    orders = jax.vmap(lambda single: jax.random.permutation(single, TOK_DEV))(subkeys).astype(jnp.int32)
    leading = orders[:, :1]
    orders = jnp.where(orders == TOK_DEV - 1, leading, orders)
    orders = orders.at[:, 0].set(TOK_DEV - 1)
    return orders[:, :MAXSEL].astype(jnp.int32)


def levels(rng, dims, cuts, low, high):
    loudness, own = 1.0, jax.random.fold_in(rng, 6)
    for position, parts in cuts:
        heights = jnp.exp(jax.random.uniform(jax.random.fold_in(own, position), (parts,), jnp.float32, low / len(cuts), high / len(cuts)))
        loudness = loudness * jnp.repeat(heights, dims[position] // parts).reshape([-1 if axis == position else 1 for axis in range(len(dims))])
    return loudness


def gaussian(key, dims, scale, limit, cuts=(), kind=jnp.bfloat16):
    values = scale * jax.random.normal(key, dims, jnp.float32)
    if cuts:
        values = values * levels(key, dims, cuts, -0.22, 0.18)
    return jnp.clip(values, -limit, limit).astype(kind)


def setup_inputs(seed: int = 0) -> dict:
    splits = jax.random.split(jax.random.key(seed), 9)
    return {
        "hidden_states": gaussian(splits[0], (TOKENS, D), 1.0, 6.0, ((0, 32), (1, 4))),
        "counts": draw_counts(jax.random.fold_in(splits[8], 71), 0),
        "selected": draw_selected(jax.random.fold_in(splits[8], 71), 0),
        "router_weight": jnp.clip(0.25 + 1.25 * jax.random.uniform(splits[3], (TOKENS,), jnp.float32) ** levels(splits[3], (TOKENS,), ((0, 32),), -0.2, 0.2), 0.25, 1.5),
        "norm_gain": jnp.clip(1.0 + 0.15 * jax.random.normal(splits[4], (D,), jnp.float32), 0.25, 1.75),
        "w_gate": gaussian(splits[5], (D, FF), D ** -0.5, 0.0625, ((0, 4), (1, 32))),
        "w_up": gaussian(splits[6], (D, FF), D ** -0.5, 0.0625, ((0, 4), (1, 32))),
        "w_down": gaussian(splits[7], (FF, D), FF ** -0.5, 0.03125, ((0, 32), (1, 4))),
    }


def reference(hidden_states, counts, selected, router_weight, norm_gain, w_gate, w_up, w_down):
    shards = hidden_states.reshape(N_CTX, TOK_DEV, D)
    picked = jnp.take_along_axis(shards, selected[:, :, None].astype(jnp.int32), axis=1).astype(jnp.float32)
    mean_sq = lax.optimization_barrier(jnp.mean(picked * picked, axis=-1, keepdims=True))
    normed = (picked * lax.rsqrt(mean_sq + 1e-05) * norm_gain.astype(jnp.float32)).astype(jnp.bfloat16)
    normed = normed.reshape(N_CTX * MAXSEL, D)
    gate = jnp.dot(normed, w_gate, preferred_element_type=jnp.float32)
    up_part = jnp.dot(normed, w_up, preferred_element_type=jnp.float32)
    hidden = (jax.nn.silu(gate) * up_part).astype(jnp.bfloat16)
    width = FF // N_CTX
    total = jnp.zeros((N_CTX * MAXSEL, D), jnp.float32)
    for group in range(N_CTX):
        partial_sum = jnp.dot(hidden[:, group * width:(group + 1) * width], w_down[group * width:(group + 1) * width], preferred_element_type=jnp.float32)
        total = total + partial_sum.astype(jnp.bfloat16).astype(jnp.float32)
    ffn_rows = lax.optimization_barrier(total.astype(jnp.bfloat16)).astype(jnp.float32)
    ffn_rows = ffn_rows.reshape(N_CTX, MAXSEL, D)
    active = (jnp.arange(MAXSEL, dtype=jnp.int32)[None, :] < counts[:, None]).astype(jnp.float32)
    weights = jnp.take_along_axis(router_weight.reshape(N_CTX, TOK_DEV), selected.astype(jnp.int32), axis=1).astype(jnp.float32) * active
    delta = ffn_rows * weights[:, :, None]
    onehot = (jnp.arange(TOK_DEV, dtype=jnp.int32)[None, :, None] == selected[:, None, :]).astype(jnp.float32)
    added = jnp.einsum('ntm,nmd->ntd', onehot, delta, precision=lax.Precision.HIGHEST)
    result = (shards.astype(jnp.float32) + added).astype(jnp.bfloat16)
    return result.reshape(N_CTX * TOK_DEV, D)
```

```python
import jax
import jax.numpy as jnp
from jax import lax
from jax.experimental import pallas as pl
from jax.experimental.pallas import tpu as pltpu
from jax.sharding import PartitionSpec as P

MESH = pl.DeviceIdType.MESH
F32 = jnp.float32
BF16 = jnp.bfloat16
N_SEM = 128


def body(hidden, counts, selected, router_weight, norm_gain, w_gate, w_up, w_down, n_ctx, n_tp):
    tok, feat = hidden.shape
    most = selected.shape[1]
    units = w_gate.shape[1]
    width = feat * n_tp
    rows = most * 2 // 3
    edge = 16
    nx, nz, ny = 4, n_ctx // 8, n_tp
    half = feat // 2
    own = ny and (nx * 2 * rows) // ny

    def kernel(counts_ref, sel_ref, rw_ref, gain_ref, hid_ref, wg_hbm, wu_hbm, wd_hbm, out_ref,
               w_gu, w_dn, sq, cnt, ztot, to_prev, to_next, from_next, from_prev,
               x_buf, part, r1, r2, h_buf, y_buf, sib_buf, q1, q2, t_buf, zr,
               tail_next, tail_prev, edge_next, edge_prev, load_sem, send_sem, recv_sem):
        ctx = lax.axis_index("ctx")
        y = lax.axis_index("tp")
        z, q = ctx // 8, ctx % 8
        x, c = q // 2, q % 2

        def at(zz, xx, cc):
            return (zz * nx + xx) * 2 + cc

        xp, xm, x2 = (x + 1) % nx, (x + nx - 1) % nx, (x + 2) % nx
        zp, zm = (z + 1) % nz, (z + nz - 1) % nz
        yp, ym, y2 = (y + 1) % ny, (y + ny - 1) % ny, (y + 2) % ny
        sib = (at(z, x, 1 - c), y)
        d_xp, d_xm = (at(z, xp, c), y), (at(z, xm, c), y)
        d_zp, d_zm = (at(zp, x, c), y), (at(zm, x, c), y)
        d_yp, d_ym = (ctx, yp), (ctx, ym)
        d_next, d_prev = ((ctx + 1) % n_ctx, y), ((ctx + n_ctx - 1) % n_ctx, y)

        loads = []
        for i, (src, dst) in enumerate((
            (wg_hbm, w_gu.at[:, pl.ds(0, units)]),
            (wu_hbm, w_gu.at[:, pl.ds(units, units)]),
            (wd_hbm, w_dn),
        )):
            load = pltpu.make_async_copy(src, dst, load_sem.at[i])
            load.start()
            loads.append(load)

        used = []

        def copy(src, dst, dev):
            i = len(used)
            d = pltpu.make_async_remote_copy(
                src_ref=src, dst_ref=dst, send_sem=send_sem.at[i], recv_sem=recv_sem.at[i],
                device_id=dev, device_id_type=MESH)
            used.append(d)
            d.start()
            return d

        row_peers = [(at(z, (q + j) % 8 // 2, (q + j) % 8 % 2), y) for j in range(1, 8)]
        z_peers = [(at((z + j) % nz, x, c), y) for j in range(1, nz)]
        y_peers = [(ctx, (y + j) % ny) for j in range(1, ny)]

        barrier = pltpu.get_barrier_semaphore()
        peers = row_peers + z_peers + y_peers + [d_next, d_prev]
        for dev in peers:
            pl.semaphore_signal(barrier, inc=1, device_id=dev, device_id_type=MESH)

        n_f = counts_ref[0].astype(F32)
        cnt[q] = jnp.full((8, 128), n_f, F32)
        hid = hid_ref[...].astype(F32)
        sq[y] = jnp.broadcast_to(jnp.sum(hid * hid, axis=-1, keepdims=True), (tok, 128))

        pl.semaphore_wait(barrier, len(peers))

        c_row = [copy(cnt.at[q], cnt.at[q], dev) for dev in row_peers]
        c_sq = [copy(sq.at[y], sq.at[y], dev) for dev in y_peers]
        for d in c_row:
            d.wait_recv()
        before = jnp.zeros((8, 128), F32)
        total = jnp.zeros((8, 128), F32)
        for j in range(8):
            before = before + cnt[j] * jnp.where(j < q, 1.0, 0.0).astype(F32)
            total = total + cnt[j]
        ztot[z] = total
        c_z = [copy(ztot.at[z], ztot.at[z], dev) for dev in z_peers]

        for d in c_sq:
            d.wait_recv()
        sums = sq[0]
        for j in range(1, ny):
            sums = sums + sq[j]
        scale = lax.rsqrt(sums[:, 0:1] / width + 1e-05)
        normed = (hid_ref[...].astype(F32) * scale * gain_ref[...]).astype(BF16)

        for d in c_z:
            d.wait_recv()
        for j in range(nz):
            before = before + ztot[j] * jnp.where(j < z, 1.0, 0.0).astype(F32)
        excess = (before - (ctx * rows).astype(F32))[0:1, 0:1]
        ids = lax.broadcasted_iota(jnp.int32, (tok, most), 0)
        rank = lax.broadcasted_iota(jnp.int32, (tok, most), 1).astype(F32)
        match = jnp.where((sel_ref[...] == ids) & (rank < n_f), 1.0, 0.0).astype(F32).astype(BF16)

        def chosen(count, offset):
            slot = lax.broadcasted_iota(jnp.int32, (count, most), 0).astype(F32) + offset
            place = lax.broadcasted_iota(jnp.int32, (count, most), 1).astype(F32) + excess
            shift = jnp.where(slot == place, 1.0, 0.0).astype(F32).astype(BF16)
            return lax.dot_general(
                shift, match, (((1,), (1,)), ((), ())), preferred_element_type=F32).astype(BF16)

        to_prev[...] = jnp.dot(chosen(edge, -edge), normed, preferred_element_type=F32).astype(BF16)
        c_prev = copy(to_prev, from_next, d_prev)
        to_next[...] = jnp.dot(chosen(edge, rows), normed, preferred_element_type=F32).astype(BF16)
        c_next = copy(to_next, from_prev, d_next)
        mine = jnp.dot(chosen(rows, 0), normed, preferred_element_type=F32)
        x_buf[0, x, c] = mine.astype(BF16)
        c_next.wait_recv()
        x_buf[0, x, c, pl.ds(0, edge)] = (
            x_buf[0, x, c, pl.ds(0, edge)].astype(F32) + from_prev[...].astype(F32)).astype(BF16)
        c_prev.wait_recv()
        x_buf[0, x, c, pl.ds(rows - edge, edge)] = (
            x_buf[0, x, c, pl.ds(rows - edge, edge)].astype(F32) + from_next[...].astype(F32)
        ).astype(BF16)

        lo, hi = pl.ds(0, half), pl.ds(half, half)
        rel = [x, xm, xp, x2]
        g_sib = [[None] * 4 for _ in range(4)]
        g_up, g_dn = [None] * 4, [None] * 4

        def spread(i):
            xb = rel[i]
            g_up[i] = copy(x_buf.at[0, xb, c], x_buf.at[3, xb, c], d_zp)
            g_dn[i] = copy(x_buf.at[0, xb, c], x_buf.at[1, xb, c], d_zm)
            share(0, i)

        def share(k, i):
            xb = rel[i]
            g_sib[k][i] = copy(x_buf.at[k, xb, c], x_buf.at[k, xb, c], sib)

        a_p = copy(x_buf.at[0, x, c], x_buf.at[0, x, c], d_xp)
        a_m = copy(x_buf.at[0, x, c], x_buf.at[0, x, c], d_xm)
        spread(0)
        a_p.wait_recv()
        b_p = copy(x_buf.at[0, xm, c, :, lo], x_buf.at[0, xm, c, :, lo], d_xp)
        a_m.wait_recv()
        b_m = copy(x_buf.at[0, xp, c, :, hi], x_buf.at[0, xp, c, :, hi], d_xm)
        spread(1)
        spread(2)
        b_p.wait_recv()
        b_m.wait_recv()
        spread(3)

        loads[0].wait()
        loads[1].wait()

        steps = (2 * units) // 256
        y_first, y_second, y_gather, y_pass = {}, {}, {}, {}

        def gate_up(k):
            for i in range(4):
                g_sib[k][i].wait_recv()

            def tile(j, carry):
                cols = pl.ds(pl.multiple_of(j * 256, 256), 256)
                res = jnp.dot(x_buf[k].reshape(nx * 2 * rows, feat), w_gu[:, cols],
                              preferred_element_type=F32)
                part[k, :, :, cols] = res.astype(BF16).reshape(ny, own, 256)
                return carry

            lax.fori_loop(0, steps, tile, 0)
            gate, up = pl.ds(0, units), pl.ds(units, units)
            y_first[k] = (copy(part.at[k, y2, :, gate], r1.at[k, 0], d_yp),
                          copy(part.at[k, y2, :, up], r1.at[k, 1], d_ym))
            y_second[k] = [copy(part.at[k, yp, :, up], r2.at[k, 0, 1], d_yp),
                           copy(part.at[k, ym, :, gate], r2.at[k, 1, 0], d_ym)]

        def combine(k):
            gate, up = pl.ds(0, units), pl.ds(units, units)
            y_first[k][0].wait_recv()
            part[k, yp, :, gate] = (
                part[k, yp, :, gate].astype(F32) + r1[k, 0].astype(F32)).astype(BF16)
            y_second[k].append(copy(part.at[k, yp, :, gate], r2.at[k, 0, 0], d_yp))
            y_first[k][1].wait_recv()
            part[k, ym, :, up] = (
                part[k, ym, :, up].astype(F32) + r1[k, 1].astype(F32)).astype(BF16)
            y_second[k].append(copy(part.at[k, ym, :, up], r2.at[k, 1, 1], d_ym))

        def activate(k):
            gate, up = pl.ds(0, units), pl.ds(units, units)
            for d in y_second[k]:
                d.wait_recv()
            g = part[k, y, :, gate].astype(F32) + r2[k, 0, 0].astype(F32) + r2[k, 1, 0].astype(F32)
            u = part[k, y, :, up].astype(F32) + r2[k, 0, 1].astype(F32) + r2[k, 1, 1].astype(F32)
            h_buf[k, y] = (g / (1.0 + jnp.exp(-g)) * u).astype(BF16)
            y_gather[k] = (copy(h_buf.at[k, y], h_buf.at[k, y], d_yp),
                           copy(h_buf.at[k, y], h_buf.at[k, y], d_ym))

        def pass_on(k):
            first, second = pl.ds(0, own // 2), pl.ds(own // 2, own // 2)
            y_gather[k][0].wait_recv()
            f_p = copy(h_buf.at[k, ym, first], h_buf.at[k, ym, first], d_yp)
            y_gather[k][1].wait_recv()
            f_m = copy(h_buf.at[k, yp, second], h_buf.at[k, yp, second], d_ym)
            y_pass[k] = (f_p, f_m)

        s_core, s_first, s_second, s_z = {}, {}, {}, {}

        def down(k):
            for d in y_pass[k]:
                d.wait_recv()

            def tile(j, carry):
                cols = pl.ds(pl.multiple_of(j * 256, 256), 256)
                res = jnp.dot(h_buf[k].reshape(nx * 2 * rows, units), w_dn[:, cols],
                              preferred_element_type=F32)
                y_buf[k, :, :, :, cols] = res.astype(BF16).reshape(nx, 2, rows, 256)
                return carry

            lax.fori_loop(0, feat // 256, tile, 0)
            s_core[k] = copy(y_buf.at[k, :, 1 - c], sib_buf.at[k], sib)

        def fold(k):
            s_core[k].wait_recv()
            for i in (3, 1, 2, 0):
                xb = rel[i]
                y_buf[k, xb, c] = (
                    y_buf[k, xb, c].astype(F32) + sib_buf[k, xb].astype(F32)).astype(BF16)
                if i == 3:
                    s_first[k] = (copy(y_buf.at[k, x2, c, :, lo], q1.at[k, 0], d_xp),
                                  copy(y_buf.at[k, x2, c, :, hi], q1.at[k, 1], d_xm))
                    s_second[k] = []
                if i == 1:
                    s_second[k].append(copy(y_buf.at[k, xm, c, :, lo], q2.at[k, 1, 0], d_xm))
                if i == 2:
                    s_second[k].append(copy(y_buf.at[k, xp, c, :, hi], q2.at[k, 0, 1], d_xp))

        def fold_on(k):
            s_first[k][0].wait_recv()
            y_buf[k, xp, c, :, lo] = (
                y_buf[k, xp, c, :, lo].astype(F32) + q1[k, 0].astype(F32)).astype(BF16)
            s_second[k].append(copy(y_buf.at[k, xp, c, :, lo], q2.at[k, 0, 0], d_xp))
            s_first[k][1].wait_recv()
            y_buf[k, xm, c, :, hi] = (
                y_buf[k, xm, c, :, hi].astype(F32) + q1[k, 1].astype(F32)).astype(BF16)
            s_second[k].append(copy(y_buf.at[k, xm, c, :, hi], q2.at[k, 1, 1], d_xm))

        def settle(k):
            for d in s_second[k]:
                d.wait_recv()
            for i, cols in enumerate((lo, hi)):
                t_buf[k, :, cols] = (
                    y_buf[k, x, c, :, cols].astype(F32) + q2[k, 0, i].astype(F32)
                    + q2[k, 1, i].astype(F32)).astype(BF16)
            if k:
                s_z[k] = copy(t_buf.at[k], zr.at[(nz - k) % nz - 1], z_peers[k - 1])

        gate_up(0)
        forward = []
        for i in range(4):
            xb = rel[i]
            g_up[i].wait_recv()
            share(3, i)
            if i in (0, 2):
                forward.append(copy(x_buf.at[3, xb, c], x_buf.at[2, xb, c], d_zp))
            g_dn[i].wait_recv()
            share(1, i)
            if i in (1, 3):
                forward.append(copy(x_buf.at[1, xb, c], x_buf.at[2, xb, c], d_zm))
        combine(0)
        gate_up(1)
        activate(0)
        for i in range(4):
            forward[i].wait_recv()
            share(2, i)
        combine(1)
        gate_up(2)
        pass_on(0)
        loads[2].wait()
        down(0)
        activate(1)
        fold(0)
        combine(2)
        gate_up(3)
        pass_on(1)
        down(1)
        fold_on(0)
        activate(2)
        settle(0)
        fold(1)
        combine(3)
        pass_on(2)
        down(2)
        fold_on(1)
        activate(3)
        settle(1)
        fold(2)
        pass_on(3)
        fold_on(2)
        down(3)
        settle(2)
        fold(3)
        fold_on(3)
        settle(3)

        ffn = t_buf[0].astype(F32)
        for k in range(1, nz):
            s_z[k].wait_recv()
        for k in range(1, nz):
            ffn = ffn + zr[k - 1].astype(F32)
        t_buf[0] = ffn.astype(BF16)
        tail_prev[...] = t_buf[0, pl.ds(0, edge)]
        e_prev = copy(tail_prev, edge_next, d_prev)
        tail_next[...] = t_buf[0, pl.ds(rows - edge, edge)]
        e_next = copy(tail_next, edge_prev, d_next)

        span = rows + 2 * edge
        slot = lax.broadcasted_iota(jnp.int32, (most, span), 1).astype(F32) - edge
        place = lax.broadcasted_iota(jnp.int32, (most, span), 0).astype(F32) + excess
        shift = jnp.where(slot == place, 1.0, 0.0).astype(F32).astype(BF16)
        pick = jnp.dot(match, shift, preferred_element_type=F32).astype(BF16)
        line = lax.broadcasted_iota(jnp.int32, (tok, tok), 0)
        col = lax.broadcasted_iota(jnp.int32, (tok, tok), 1)
        weight = jnp.sum(jnp.where(line == col, rw_ref[...], 0.0), axis=-1, keepdims=True)
        e_prev.wait_recv()
        e_next.wait_recv()
        rows_all = jnp.concatenate([edge_prev[...], t_buf[0], edge_next[...]], axis=0)
        added = jnp.dot(pick, rows_all, preferred_element_type=F32)
        out_ref[...] = (hid_ref[...].astype(F32) + weight * added).astype(BF16)

        for d in used:
            d.wait_send()

    vmem = pl.BlockSpec(memory_space=pltpu.VMEM)
    hbm = pl.BlockSpec(memory_space=pl.ANY)
    blocks = (nx, 2, rows, feat)
    return pl.pallas_call(
        kernel,
        out_shape=jax.ShapeDtypeStruct((tok, feat), BF16),
        in_specs=[pl.BlockSpec(memory_space=pltpu.SMEM), vmem, vmem, vmem, vmem, hbm, hbm, hbm],
        out_specs=vmem,
        scratch_shapes=[
            pltpu.VMEM((feat, 2 * units), BF16),
            pltpu.VMEM((units, feat), BF16),
            pltpu.VMEM((ny, tok, 128), F32),
            pltpu.VMEM((8, 8, 128), F32),
            pltpu.VMEM((nz, 8, 128), F32),
            pltpu.VMEM((edge, feat), BF16),
            pltpu.VMEM((edge, feat), BF16),
            pltpu.VMEM((edge, feat), BF16),
            pltpu.VMEM((edge, feat), BF16),
            pltpu.VMEM((nz,) + blocks, BF16),
            pltpu.VMEM((nz, ny, own, 2 * units), BF16),
            pltpu.VMEM((nz, 2, own, units), BF16),
            pltpu.VMEM((nz, 2, 2, own, units), BF16),
            pltpu.VMEM((nz, ny, own, units), BF16),
            pltpu.VMEM((nz,) + blocks, BF16),
            pltpu.VMEM((nz, nx, rows, feat), BF16),
            pltpu.VMEM((nz, 2, rows, half), BF16),
            pltpu.VMEM((nz, 2, 2, rows, half), BF16),
            pltpu.VMEM((nz, rows, feat), BF16),
            pltpu.VMEM((nz - 1, rows, feat), BF16),
            pltpu.VMEM((edge, feat), BF16),
            pltpu.VMEM((edge, feat), BF16),
            pltpu.VMEM((edge, feat), BF16),
            pltpu.VMEM((edge, feat), BF16),
            pltpu.SemaphoreType.DMA((3,)),
            pltpu.SemaphoreType.DMA((N_SEM,)),
            pltpu.SemaphoreType.DMA((N_SEM,)),
        ],
        compiler_params=pltpu.CompilerParams(
            collective_id=0, has_side_effects=True, vmem_limit_bytes=56 * 1024 * 1024),
    )(counts, selected, router_weight.reshape(1, tok), norm_gain.reshape(1, feat), hidden,
      w_gate, w_up, w_down)


def solution(mesh):
    n_ctx, n_tp = mesh.shape["ctx"], mesh.shape["tp"]
    placed = (
        P("ctx", "tp"),
        P("ctx"),
        P("ctx", None),
        P("ctx"),
        P("tp"),
        P("tp", "ctx"),
        P("tp", "ctx"),
        P("ctx", "tp"),
    )

    def step(*args):
        return body(*args, n_ctx, n_tp)

    return jax.shard_map(
        step, mesh=mesh, in_specs=placed, out_specs=P("ctx", "tp"), check_vma=False
    )
```

```python
import jax
import jax.numpy as jnp
from jax import lax
from jax.experimental import pallas as pl
from jax.experimental.pallas import tpu as pltpu
from jax.sharding import PartitionSpec as P

MESH = pl.DeviceIdType.MESH
F32 = jnp.float32
BF16 = jnp.bfloat16
N_SEM = 224


def body(hidden, counts, selected, router_weight, norm_gain, w_gate, w_up, w_down, n_ctx, n_tp):
    tok, feat = hidden.shape
    most = selected.shape[1]
    units = w_gate.shape[1]
    width = feat * n_tp
    rows = most * 2 // 3
    edge = 16
    nx, nz, ny = 4, n_ctx // 8, n_tp
    fixed = 16

    def kernel(counts_ref, sel_ref, rw_ref, gain_ref, hid_ref, wg_hbm, wu_hbm, wd_hbm, out_ref,
               w_gu, w_dn, sq, cnt, ztot, to_prev, to_next, from_next, from_prev,
               x_buf, part, r1, r2, h_buf, y_buf, sib_buf, q1, t_buf, zr,
               edge_next, edge_prev, load_sem, send_sem, recv_sem):
        ctx = lax.axis_index("ctx")
        y = lax.axis_index("tp")
        z, q = ctx // 8, ctx % 8
        x, c = q // 2, q % 2

        def at(zz, xx, cc):
            return (zz * nx + xx) * 2 + cc

        xp, xm, x2 = (x + 1) % nx, (x + nx - 1) % nx, (x + 2) % nx
        zp, zm = (z + 1) % nz, (z + nz - 1) % nz
        yp, ym, y2 = (y + 1) % ny, (y + ny - 1) % ny, (y + 2) % ny
        sib = (at(z, x, 1 - c), y)
        d_xp, d_xm = (at(z, xp, c), y), (at(z, xm, c), y)
        d_zp, d_zm = (at(zp, x, c), y), (at(zm, x, c), y)
        d_yp, d_ym = (ctx, yp), (ctx, ym)
        d_next, d_prev = ((ctx + 1) % n_ctx, y), ((ctx + n_ctx - 1) % n_ctx, y)

        loads = []
        for i, (src, dst) in enumerate((
            (wg_hbm, w_gu.at[:, pl.ds(0, units)]),
            (wu_hbm, w_gu.at[:, pl.ds(units, units)]),
            (wd_hbm, w_dn),
        )):
            load = pltpu.make_async_copy(src, dst, load_sem.at[i])
            load.start()
            loads.append(load)

        used = []

        def copy(src, dst, dev):
            i = len(used)
            d = pltpu.make_async_remote_copy(
                src_ref=src, dst_ref=dst, send_sem=send_sem.at[i], recv_sem=recv_sem.at[i],
                device_id=dev, device_id_type=MESH)
            used.append(d)
            d.start()
            return d

        row_peers = [(at(z, (q + j) % 8 // 2, (q + j) % 8 % 2), y) for j in range(1, 8)]
        x_peers = [(at(z, (x + j) % nx, c), y) for j in range(1, nx)]
        z_peers = [(at((z + j) % nz, x, c), y) for j in range(1, nz)]
        y_peers = [(ctx, (y + j) % ny) for j in range(1, ny)]

        barrier = pltpu.get_barrier_semaphore()
        peers = row_peers + z_peers + y_peers + [d_next, d_prev]
        for dev in peers:
            pl.semaphore_signal(barrier, inc=1, device_id=dev, device_id_type=MESH)

        n_f = counts_ref[0].astype(F32)
        cnt[q] = jnp.full((8, 128), n_f, F32)
        hid = hid_ref[...].astype(F32)
        diagonal = (lax.broadcasted_iota(jnp.int32, (tok, 128), 0)
                    == lax.broadcasted_iota(jnp.int32, (tok, 128), 1))
        squares = jnp.sum(hid * hid, axis=-1, keepdims=True)
        sq[y] = jnp.broadcast_to(
            jnp.sum(jnp.where(diagonal, squares, 0.0), axis=0, keepdims=True), (8, 128))
        ids = lax.broadcasted_iota(jnp.int32, (tok, most), 0)
        rank = lax.broadcasted_iota(jnp.int32, (tok, most), 1).astype(F32)
        match = jnp.where((sel_ref[...] == ids) & (rank < n_f), 1.0, 0.0).astype(F32).astype(BF16)

        def chosen(count, offset, first, excess):
            slot = lax.broadcasted_iota(jnp.int32, (count, most), 0).astype(F32) + offset
            place = lax.broadcasted_iota(jnp.int32, (count, most), 1).astype(F32)
            here = (place < fixed) if first else (place >= fixed)
            shift = jnp.where((slot == place + excess) & here, 1.0, 0.0).astype(F32).astype(BF16)
            return lax.dot_general(
                shift, match, (((1,), (1,)), ((), ())), preferred_element_type=F32).astype(BF16)

        pl.semaphore_wait(barrier, len(peers))

        c_sq = [copy(sq.at[y], sq.at[y], dev) for dev in y_peers]
        c_row = [copy(cnt.at[q], cnt.at[q], dev) for dev in row_peers]
        for d in c_sq:
            d.wait_recv()
        sums = sq[0]
        for j in range(1, ny):
            sums = sums + sq[j]
        scale = lax.rsqrt(sums / width + 1e-05)[0:1]
        scale = jnp.sum(jnp.where(diagonal, scale, 0.0), axis=-1, keepdims=True)
        normed = (hid_ref[...].astype(F32) * scale * gain_ref[...]).astype(BF16)

        parts = ((0, fixed), (fixed, rows - fixed))
        rel = [x, xm, xp, x2]
        g_x, g_up, g_dn, g_sib = {}, {}, {}, {}

        def spread(p, i):
            xb, rs = rel[i], pl.ds(*parts[p])
            g_up[p, i] = copy(x_buf.at[0, xb, c, rs], x_buf.at[3, xb, c, rs], d_zp)
            g_dn[p, i] = copy(x_buf.at[0, xb, c, rs], x_buf.at[1, xb, c, rs], d_zm)
            g_sib[0, p, i] = copy(x_buf.at[0, xb, c, rs], x_buf.at[0, xb, c, rs], sib)

        def share(k, p):
            rs = pl.ds(*parts[p])
            g_sib[k, p] = copy(x_buf.at[k, :, c, rs], x_buf.at[k, :, c, rs], sib)

        def offer(p):
            rs = pl.ds(*parts[p])
            g_x[p] = [copy(x_buf.at[0, x, c, rs], x_buf.at[0, x, c, rs], dev) for dev in x_peers]
            spread(p, 0)

        def take(p, n):
            i, j = ((1, 0), (2, 2), (3, 1))[n]
            g_x[p][j].wait_recv()
            spread(p, i)

        x_buf[0, x, c, pl.ds(0, fixed)] = jnp.dot(
            chosen(fixed, 0, True, 0.0), normed, preferred_element_type=F32).astype(BF16)
        offer(0)

        for d in c_row:
            d.wait_recv()
        before = jnp.zeros((8, 128), F32)
        total = jnp.zeros((8, 128), F32)
        for j in range(8):
            before = before + cnt[j] * jnp.where(j < q, 1.0, 0.0).astype(F32)
            total = total + cnt[j]
        ztot[z] = total
        c_z = [copy(ztot.at[z], ztot.at[z], dev) for dev in z_peers]

        take(0, 0)
        take(0, 1)
        take(0, 2)
        loads[0].wait()
        loads[1].wait()
        for d in c_z:
            d.wait_recv()
        for j in range(nz):
            before = before + ztot[j] * jnp.where(j < z, 1.0, 0.0).astype(F32)
        excess = (before - (ctx * rows).astype(F32))[0:1, 0:1]
        to_prev[...] = jnp.dot(
            chosen(edge, 0, False, excess), normed, preferred_element_type=F32).astype(BF16)
        c_prev = copy(to_prev, from_next, d_prev)
        to_next[...] = jnp.dot(
            chosen(edge, rows, False, excess), normed, preferred_element_type=F32).astype(BF16)
        c_next = copy(to_next, from_prev, d_next)
        x_buf[0, x, c, pl.ds(fixed, rows - fixed)] = jnp.dot(
            chosen(rows - fixed, fixed, False, excess), normed, preferred_element_type=F32
        ).astype(BF16)

        def settle_rows():
            for d, got, r0 in ((c_next, from_prev, fixed), (c_prev, from_next, rows - edge)):
                d.wait_recv()
                x_buf[0, x, c, pl.ds(r0, edge)] = (
                    x_buf[0, x, c, pl.ds(r0, edge)].astype(F32) + got[...].astype(F32)
                ).astype(BF16)
            offer(1)

        subs = ((0, 0, 16), (1, 0, 16), (3, 0, 16), (2, 0, 16), (0, 16, 32), (2, 16, 32), (3, 16, 32), (1, 16, 32))
        waited = set()
        gate, up = pl.ds(0, units), pl.ds(units, units)
        steps = (2 * units) // 256
        y_first, y_second, y_gather, y_pass = {}, {}, {}, {}

        def gate_up(s):
            k, r0, nr = subs[s]
            rs = pl.ds(r0, nr)
            for p, (first, count) in enumerate(parts):
                if first < r0 + nr and r0 < first + count and (k, p) not in waited:
                    waited.add((k, p))
                    for d in [g_sib[0, p, i] for i in range(4)] if k == 0 else [g_sib[k, p]]:
                        d.wait_recv()

            def tile(j, carry):
                cols = pl.ds(pl.multiple_of(j * 256, 256), 256)
                res = jnp.dot(x_buf[k, :, :, rs].reshape(nx * 2 * nr, feat), w_gu[:, cols],
                              preferred_element_type=F32)
                part[k, :, :, rs, cols] = res.astype(BF16).reshape(ny, 2, nr, 256)
                return carry

            lax.fori_loop(0, steps, tile, 0)
            y_first[s] = (copy(part.at[k, y2, :, rs, gate], r1.at[k, 0, :, rs], d_yp),
                          copy(part.at[k, y2, :, rs, up], r1.at[k, 1, :, rs], d_ym))
            y_second[s] = [copy(part.at[k, yp, :, rs, up], r2.at[k, 0, 1, :, rs], d_yp),
                           copy(part.at[k, ym, :, rs, gate], r2.at[k, 1, 0, :, rs], d_ym)]

        def combine(s):
            k, r0, nr = subs[s]
            rs = pl.ds(r0, nr)
            y_first[s][0].wait_recv()
            part[k, yp, :, rs, gate] = (
                part[k, yp, :, rs, gate].astype(F32) + r1[k, 0, :, rs].astype(F32)).astype(BF16)
            y_second[s].append(copy(part.at[k, yp, :, rs, gate], r2.at[k, 0, 0, :, rs], d_yp))
            y_first[s][1].wait_recv()
            part[k, ym, :, rs, up] = (
                part[k, ym, :, rs, up].astype(F32) + r1[k, 1, :, rs].astype(F32)).astype(BF16)
            y_second[s].append(copy(part.at[k, ym, :, rs, up], r2.at[k, 1, 1, :, rs], d_ym))

        def activate(s):
            k, r0, nr = subs[s]
            rs = pl.ds(r0, nr)
            for d in y_second[s]:
                d.wait_recv()
            g = (part[k, y, :, rs, gate].astype(F32) + r2[k, 0, 0, :, rs].astype(F32)
                 + r2[k, 1, 0, :, rs].astype(F32))
            u = (part[k, y, :, rs, up].astype(F32) + r2[k, 0, 1, :, rs].astype(F32)
                 + r2[k, 1, 1, :, rs].astype(F32))
            h_buf[k, y, :, rs] = (g / (1.0 + jnp.exp(-g)) * u).astype(BF16)
            mine = h_buf.at[k, y, :, rs]
            y_gather[s] = (copy(mine, mine, d_yp), copy(mine, mine, d_ym))

        def pass_on(s):
            k, r0, nr = subs[s]
            rs = pl.ds(r0, nr)
            y_gather[s][0].wait_recv()
            left = h_buf.at[k, ym, 0, rs]
            f_p = copy(left, left, d_yp)
            y_gather[s][1].wait_recv()
            right = h_buf.at[k, yp, 1, rs]
            f_m = copy(right, right, d_ym)
            y_pass[s] = (f_p, f_m)

        s_core, s_x, s_z = {}, {}, {}

        def down(s):
            k, r0, nr = subs[s]
            rs = pl.ds(r0, nr)
            for d in y_pass[s]:
                d.wait_recv()

            def tile(j, carry):
                cols = pl.ds(pl.multiple_of(j * 256, 256), 256)
                res = jnp.dot(h_buf[k, :, :, rs].reshape(nx * 2 * nr, units), w_dn[:, cols],
                              preferred_element_type=F32)
                y_buf[k, :, :, rs, cols] = res.astype(BF16).reshape(nx, 2, nr, 256)
                return carry

            lax.fori_loop(0, feat // 256, tile, 0)
            s_core[s] = copy(y_buf.at[k, :, 1 - c, rs], sib_buf.at[k, :, rs], sib)

        def fold(s):
            k, r0, nr = subs[s]
            rs = pl.ds(r0, nr)
            s_core[s].wait_recv()
            s_x[s] = []
            for j in (2, 1, 3, 0):
                xb = (x + j) % nx
                y_buf[k, xb, c, rs] = (
                    y_buf[k, xb, c, rs].astype(F32) + sib_buf[k, xb, rs].astype(F32)).astype(BF16)
                if j:
                    s_x[s].append(copy(y_buf.at[k, xb, c, rs], q1.at[k, nx - j - 1, rs],
                                       x_peers[j - 1]))

        def settle(s):
            k, r0, nr = subs[s]
            rs = pl.ds(r0, nr)
            for d in s_x[s]:
                d.wait_recv()
            t_buf[k, rs] = (
                y_buf[k, x, c, rs].astype(F32) + q1[k, 0, rs].astype(F32)
                + q1[k, 1, rs].astype(F32) + q1[k, 2, rs].astype(F32)).astype(BF16)
            if k:
                s_z[s] = copy(t_buf.at[k, rs], zr.at[(nz - k) % nz - 1, rs], z_peers[k - 1])

        def z_take(p, i):
            xb, rs = rel[i], pl.ds(*parts[p])
            g_up[p, i].wait_recv()
            g_dn[p, i].wait_recv()
            k, dev = ((3, d_zp), (1, d_zm))[i % 2]
            forward[p].append(copy(x_buf.at[k, xb, c, rs], x_buf.at[2, xb, c, rs], dev))
            if i == 3:
                share(1, p)
                share(3, p)

        def z_last(p):
            for d in forward[p]:
                d.wait_recv()
            share(2, p)

        forward = ([], [])
        z_take(0, 0)
        gate_up(0)
        settle_rows()
        z_take(0, 1)
        z_take(0, 2)
        z_take(0, 3)
        combine(0)
        gate_up(2)
        activate(0)
        take(1, 0)
        gate_up(1)
        take(1, 1)
        z_last(0)
        combine(2)
        take(1, 2)
        gate_up(3)
        gate_up(4)
        combine(1)
        activate(2)
        z_take(1, 0)
        z_take(1, 1)
        z_take(1, 2)
        z_take(1, 3)
        combine(3)
        gate_up(7)
        pass_on(0)
        activate(3)
        gate_up(6)
        pass_on(3)
        activate(1)
        combine(4)
        pass_on(1)
        combine(7)
        loads[2].wait()
        down(0)
        pass_on(2)
        down(3)
        z_last(1)
        fold(0)
        activate(4)
        down(1)
        activate(7)
        down(2)
        combine(6)
        pass_on(4)
        fold(3)
        gate_up(5)
        fold(2)
        fold(1)
        pass_on(7)
        down(4)
        fold(4)
        activate(6)
        combine(5)
        down(7)
        settle(3)
        pass_on(6)
        fold(7)
        activate(5)
        down(6)
        pass_on(5)
        settle(2)
        settle(4)
        fold(6)
        down(5)
        fold(5)
        settle(7)
        settle(1)
        settle(0)
        settle(6)
        settle(5)

        for s in s_z:
            s_z[s].wait_recv()
        ffn = t_buf[0].astype(F32)
        for k in range(1, nz):
            ffn = ffn + zr[k - 1].astype(F32)
        t_buf[0] = ffn.astype(BF16)
        e_prev = copy(t_buf.at[0, pl.ds(fixed, edge)], edge_next, d_prev)
        e_next = copy(t_buf.at[0, pl.ds(rows - edge, edge)], edge_prev, d_next)
        span = rows + 2 * edge
        slot = lax.broadcasted_iota(jnp.int32, (most, span), 1).astype(F32)
        place = lax.broadcasted_iota(jnp.int32, (most, span), 0).astype(F32)
        aim = jnp.where(place < fixed, place, place + excess + fixed)
        shift = jnp.where(slot == aim, 1.0, 0.0).astype(F32).astype(BF16)
        pick = jnp.dot(match, shift, preferred_element_type=F32).astype(BF16)
        line = lax.broadcasted_iota(jnp.int32, (tok, tok), 0)
        col = lax.broadcasted_iota(jnp.int32, (tok, tok), 1)
        weight = jnp.sum(jnp.where(line == col, rw_ref[...], 0.0), axis=-1, keepdims=True)
        e_prev.wait_recv()
        e_next.wait_recv()
        rows_all = jnp.concatenate(
            [t_buf[0, pl.ds(0, fixed)], edge_prev[...], t_buf[0, pl.ds(fixed, rows - fixed)],
             edge_next[...]], axis=0)
        added = jnp.dot(pick, rows_all, preferred_element_type=F32)
        out_ref[...] = (hid_ref[...].astype(F32) + weight * added).astype(BF16)

        for d in used:
            d.wait_send()

    vmem = pl.BlockSpec(memory_space=pltpu.VMEM)
    hbm = pl.BlockSpec(memory_space=pl.ANY)
    blocks = (nx, 2, rows, feat)
    return pl.pallas_call(
        kernel,
        out_shape=jax.ShapeDtypeStruct((tok, feat), BF16),
        in_specs=[pl.BlockSpec(memory_space=pltpu.SMEM), vmem, vmem, vmem, vmem, hbm, hbm, hbm],
        out_specs=vmem,
        scratch_shapes=[
            pltpu.VMEM((feat, 2 * units), BF16),
            pltpu.VMEM((units, feat), BF16),
            pltpu.VMEM((ny, 8, 128), F32),
            pltpu.VMEM((8, 8, 128), F32),
            pltpu.VMEM((nz, 8, 128), F32),
            pltpu.VMEM((edge, feat), BF16),
            pltpu.VMEM((edge, feat), BF16),
            pltpu.VMEM((edge, feat), BF16),
            pltpu.VMEM((edge, feat), BF16),
            pltpu.VMEM((nz,) + blocks, BF16),
            pltpu.VMEM((nz, ny, 2, rows, 2 * units), BF16),
            pltpu.VMEM((nz, 2, 2, rows, units), BF16),
            pltpu.VMEM((nz, 2, 2, 2, rows, units), BF16),
            pltpu.VMEM((nz, ny, 2, rows, units), BF16),
            pltpu.VMEM((nz,) + blocks, BF16),
            pltpu.VMEM((nz, nx, rows, feat), BF16),
            pltpu.VMEM((nz, nx - 1, rows, feat), BF16),
            pltpu.VMEM((nz, rows, feat), BF16),
            pltpu.VMEM((nz - 1, rows, feat), BF16),
            pltpu.VMEM((edge, feat), BF16),
            pltpu.VMEM((edge, feat), BF16),
            pltpu.SemaphoreType.DMA((3,)),
            pltpu.SemaphoreType.DMA((N_SEM,)),
            pltpu.SemaphoreType.DMA((N_SEM,)),
        ],
        compiler_params=pltpu.CompilerParams(
            collective_id=0, has_side_effects=True, vmem_limit_bytes=56 * 1024 * 1024),
    )(counts, selected, router_weight.reshape(1, tok), norm_gain.reshape(1, feat), hidden,
      w_gate, w_up, w_down)


def solution(mesh):
    n_ctx, n_tp = mesh.shape["ctx"], mesh.shape["tp"]
    placed = (
        P("ctx", "tp"),
        P("ctx"),
        P("ctx", None),
        P("ctx"),
        P("tp"),
        P("tp", "ctx"),
        P("tp", "ctx"),
        P("ctx", "tp"),
    )

    def step(*args):
        return body(*args, n_ctx, n_tp)

    return jax.shard_map(
        step, mesh=mesh, in_specs=placed, out_specs=P("ctx", "tp"), check_vma=False
    )
```

```python
import jax
import jax.numpy as jnp
from jax import lax
from jax.experimental import pallas as pl
from jax.experimental.pallas import tpu as pltpu
from jax.sharding import PartitionSpec as P

MESH = pl.DeviceIdType.MESH
F32 = jnp.float32
BF16 = jnp.bfloat16
N_SEM = 224


def body(hidden, counts, selected, router_weight, norm_gain, w_gate, w_up, w_down, n_ctx, n_tp):
    tok, feat = hidden.shape
    most = selected.shape[1]
    units = w_gate.shape[1]
    width = feat * n_tp
    rows = most * 2 // 3
    edge = 16
    nx, nz, ny = 4, n_ctx // 8, n_tp
    fixed = 16

    def kernel(counts_ref, sel_ref, rw_ref, gain_ref, hid_ref, wg_hbm, wu_hbm, wd_hbm, out_ref,
               w_gu, w_dn, sq, cnt, ztot, to_prev, to_next, from_next, from_prev,
               x_buf, part, r1, r2, h_buf, y_buf, sib_buf, q1, t_buf, zr,
               edge_next, edge_prev, load_sem, send_sem, recv_sem):
        ctx = lax.axis_index("ctx")
        y = lax.axis_index("tp")
        z, q = ctx // 8, ctx % 8
        x, c = q // 2, q % 2

        def at(zz, xx, cc):
            return (zz * nx + xx) * 2 + cc

        xp, xm, x2 = (x + 1) % nx, (x + nx - 1) % nx, (x + 2) % nx
        zp, zm = (z + 1) % nz, (z + nz - 1) % nz
        yp, ym, y2 = (y + 1) % ny, (y + ny - 1) % ny, (y + 2) % ny
        sib = (at(z, x, 1 - c), y)
        d_xp, d_xm = (at(z, xp, c), y), (at(z, xm, c), y)
        d_zp, d_zm = (at(zp, x, c), y), (at(zm, x, c), y)
        d_yp, d_ym = (ctx, yp), (ctx, ym)
        d_next, d_prev = ((ctx + 1) % n_ctx, y), ((ctx + n_ctx - 1) % n_ctx, y)

        loads = []
        for i, (src, dst) in enumerate((
            (wg_hbm, w_gu.at[:, pl.ds(0, units)]),
            (wu_hbm, w_gu.at[:, pl.ds(units, units)]),
            (wd_hbm, w_dn),
        )):
            load = pltpu.make_async_copy(src, dst, load_sem.at[i])
            load.start()
            loads.append(load)

        used = []

        def copy(src, dst, dev):
            i = len(used)
            d = pltpu.make_async_remote_copy(
                src_ref=src, dst_ref=dst, send_sem=send_sem.at[i], recv_sem=recv_sem.at[i],
                device_id=dev, device_id_type=MESH)
            used.append(d)
            d.start()
            return d

        row_peers = [(at(z, (q + j) % 8 // 2, (q + j) % 8 % 2), y) for j in range(1, 8)]
        x_peers = [(at(z, (x + j) % nx, c), y) for j in range(1, nx)]
        z_peers = [(at((z + j) % nz, x, c), y) for j in range(1, nz)]
        y_peers = [(ctx, (y + j) % ny) for j in range(1, ny)]

        barrier = pltpu.get_barrier_semaphore()
        peers = row_peers + z_peers + y_peers + [d_next, d_prev]
        for dev in peers:
            pl.semaphore_signal(barrier, inc=1, device_id=dev, device_id_type=MESH)

        n_f = counts_ref[0].astype(F32)
        cnt[q] = jnp.full((8, 128), n_f, F32)
        hid = hid_ref[...].astype(F32)
        diagonal = (lax.broadcasted_iota(jnp.int32, (tok, 128), 0)
                    == lax.broadcasted_iota(jnp.int32, (tok, 128), 1))
        squares = jnp.sum(hid * hid, axis=-1, keepdims=True)
        sq[y] = jnp.broadcast_to(
            jnp.sum(jnp.where(diagonal, squares, 0.0), axis=0, keepdims=True), (8, 128))
        ids = lax.broadcasted_iota(jnp.int32, (tok, most), 0)
        rank = lax.broadcasted_iota(jnp.int32, (tok, most), 1).astype(F32)
        match = jnp.where((sel_ref[...] == ids) & (rank < n_f), 1.0, 0.0).astype(F32).astype(BF16)

        def chosen(count, offset, first, excess):
            slot = lax.broadcasted_iota(jnp.int32, (count, most), 0).astype(F32) + offset
            place = lax.broadcasted_iota(jnp.int32, (count, most), 1).astype(F32)
            here = (place < fixed) if first else (place >= fixed)
            shift = jnp.where((slot == place + excess) & here, 1.0, 0.0).astype(F32).astype(BF16)
            return lax.dot_general(
                shift, match, (((1,), (1,)), ((), ())), preferred_element_type=F32).astype(BF16)

        pl.semaphore_wait(barrier, len(peers))

        c_sq = [copy(sq.at[y], sq.at[y], dev) for dev in y_peers]
        c_row = [copy(cnt.at[q], cnt.at[q], dev) for dev in row_peers]
        for d in c_sq:
            d.wait_recv()
        sums = sq[0]
        for j in range(1, ny):
            sums = sums + sq[j]
        scale = lax.rsqrt(sums / width + 1e-05)[0:1]
        scale = jnp.sum(jnp.where(diagonal, scale, 0.0), axis=-1, keepdims=True)
        normed = (hid_ref[...].astype(F32) * scale * gain_ref[...]).astype(BF16)

        parts = ((0, fixed), (fixed, rows - fixed))
        rel = [x, xm, xp, x2]
        g_x, g_up, g_dn, g_sib = {}, {}, {}, {}

        def spread(p, i):
            xb, rs = rel[i], pl.ds(*parts[p])
            g_up[p, i] = copy(x_buf.at[0, xb, c, rs], x_buf.at[3, xb, c, rs], d_zp)
            g_dn[p, i] = copy(x_buf.at[0, xb, c, rs], x_buf.at[1, xb, c, rs], d_zm)
            g_sib[0, p, i] = copy(x_buf.at[0, xb, c, rs], x_buf.at[0, xb, c, rs], sib)

        def share(k, p):
            rs = pl.ds(*parts[p])
            g_sib[k, p] = copy(x_buf.at[k, :, c, rs], x_buf.at[k, :, c, rs], sib)

        def offer(p):
            rs = pl.ds(*parts[p])
            g_x[p] = [copy(x_buf.at[0, x, c, rs], x_buf.at[0, x, c, rs], dev) for dev in x_peers]
            spread(p, 0)

        def take(p, n):
            i, j = ((1, 0), (2, 2), (3, 1))[n]
            g_x[p][j].wait_recv()
            spread(p, i)

        x_buf[0, x, c, pl.ds(0, fixed)] = jnp.dot(
            chosen(fixed, 0, True, 0.0), normed, preferred_element_type=F32).astype(BF16)
        offer(0)

        for d in c_row:
            d.wait_recv()
        before = jnp.zeros((8, 128), F32)
        total = jnp.zeros((8, 128), F32)
        for j in range(8):
            before = before + cnt[j] * jnp.where(j < q, 1.0, 0.0).astype(F32)
            total = total + cnt[j]
        ztot[z] = total
        c_z = [copy(ztot.at[z], ztot.at[z], dev) for dev in z_peers]

        take(0, 0)
        take(0, 1)
        take(0, 2)
        loads[0].wait()
        loads[1].wait()
        for d in c_z:
            d.wait_recv()
        for j in range(nz):
            before = before + ztot[j] * jnp.where(j < z, 1.0, 0.0).astype(F32)
        excess = (before - (ctx * rows).astype(F32))[0:1, 0:1]
        to_prev[...] = jnp.dot(
            chosen(edge, 0, False, excess), normed, preferred_element_type=F32).astype(BF16)
        c_prev = copy(to_prev, from_next, d_prev)
        to_next[...] = jnp.dot(
            chosen(edge, rows, False, excess), normed, preferred_element_type=F32).astype(BF16)
        c_next = copy(to_next, from_prev, d_next)
        x_buf[0, x, c, pl.ds(fixed, rows - fixed)] = jnp.dot(
            chosen(rows - fixed, fixed, False, excess), normed, preferred_element_type=F32
        ).astype(BF16)

        def settle_rows():
            for d, got, r0 in ((c_next, from_prev, fixed), (c_prev, from_next, rows - edge)):
                d.wait_recv()
                x_buf[0, x, c, pl.ds(r0, edge)] = (
                    x_buf[0, x, c, pl.ds(r0, edge)].astype(F32) + got[...].astype(F32)
                ).astype(BF16)
            offer(1)

        subs = ((0, 0, 16), (1, 0, 16), (3, 0, 16), (2, 0, 16), (0, 16, 32), (2, 16, 32), (3, 16, 32), (1, 16, 32))
        direct = (0,)
        waited = set()
        gate, up = pl.ds(0, units), pl.ds(units, units)
        steps = (2 * units) // 256
        y_first, y_second, y_gather, y_pass = {}, {}, {}, {}

        def gate_up(s):
            k, r0, nr = subs[s]
            rs = pl.ds(r0, nr)
            for p, (first, count) in enumerate(parts):
                if first < r0 + nr and r0 < first + count and (k, p) not in waited:
                    waited.add((k, p))
                    for d in [g_sib[0, p, i] for i in range(4)] if k == 0 else [g_sib[k, p]]:
                        d.wait_recv()

            for j in range(steps):
                cols = pl.ds(j * 256, 256)
                res = jnp.dot(x_buf[k, :, :, rs].reshape(nx * 2 * nr, feat), w_gu[:, cols],
                              preferred_element_type=F32)
                part[k, :, :, rs, cols] = res.astype(BF16).reshape(ny, 2, nr, 256)
            if s in direct:
                y_second[s] = [
                    copy(part.at[k, owner, :, rs, cols], place.at[:, rs], dev)
                    for owner, dev, places in (
                        (y2, (ctx, y2), (r1.at[k, 0], r1.at[k, 1])),
                        (yp, d_yp, (r2.at[k, 0, 0], r2.at[k, 0, 1])),
                        (ym, d_ym, (r2.at[k, 1, 0], r2.at[k, 1, 1])))
                    for cols, place in zip((gate, up), places)]
                return
            y_first[s] = (copy(part.at[k, y2, :, rs, gate], r1.at[k, 0, :, rs], d_yp),
                          copy(part.at[k, y2, :, rs, up], r1.at[k, 1, :, rs], d_ym))
            y_second[s] = [copy(part.at[k, yp, :, rs, up], r2.at[k, 0, 1, :, rs], d_yp),
                           copy(part.at[k, ym, :, rs, gate], r2.at[k, 1, 0, :, rs], d_ym)]

        def combine(s):
            k, r0, nr = subs[s]
            rs = pl.ds(r0, nr)
            y_first[s][0].wait_recv()
            part[k, yp, :, rs, gate] = (
                part[k, yp, :, rs, gate].astype(F32) + r1[k, 0, :, rs].astype(F32)).astype(BF16)
            y_second[s].append(copy(part.at[k, yp, :, rs, gate], r2.at[k, 0, 0, :, rs], d_yp))
            y_first[s][1].wait_recv()
            part[k, ym, :, rs, up] = (
                part[k, ym, :, rs, up].astype(F32) + r1[k, 1, :, rs].astype(F32)).astype(BF16)
            y_second[s].append(copy(part.at[k, ym, :, rs, up], r2.at[k, 1, 1, :, rs], d_ym))

        def activate(s):
            k, r0, nr = subs[s]
            rs = pl.ds(r0, nr)
            for d in y_second[s]:
                d.wait_recv()
            g = (part[k, y, :, rs, gate].astype(F32) + r2[k, 0, 0, :, rs].astype(F32)
                 + r2[k, 1, 0, :, rs].astype(F32))
            u = (part[k, y, :, rs, up].astype(F32) + r2[k, 0, 1, :, rs].astype(F32)
                 + r2[k, 1, 1, :, rs].astype(F32))
            if s in direct:
                g = g + r1[k, 0, :, rs].astype(F32)
                u = u + r1[k, 1, :, rs].astype(F32)
            h_buf[k, y, :, rs] = (g / (1.0 + jnp.exp(-g)) * u).astype(BF16)
            mine = h_buf.at[k, y, :, rs]
            y_gather[s] = (copy(mine, mine, d_yp), copy(mine, mine, d_ym))
            if s in direct:
                y_pass[s] = y_gather[s] + (copy(mine, mine, (ctx, y2)),)

        def pass_on(s):
            k, r0, nr = subs[s]
            rs = pl.ds(r0, nr)
            y_gather[s][0].wait_recv()
            left = h_buf.at[k, ym, 0, rs]
            f_p = copy(left, left, d_yp)
            y_gather[s][1].wait_recv()
            right = h_buf.at[k, yp, 1, rs]
            f_m = copy(right, right, d_ym)
            y_pass[s] = (f_p, f_m)

        s_core, s_x, s_z = {}, {}, {}

        def down(s):
            k, r0, nr = subs[s]
            rs = pl.ds(r0, nr)
            for d in y_pass[s]:
                d.wait_recv()

            for j in range(feat // 256):
                cols = pl.ds(j * 256, 256)
                res = jnp.dot(h_buf[k, :, :, rs].reshape(nx * 2 * nr, units), w_dn[:, cols],
                              preferred_element_type=F32)
                y_buf[k, :, :, rs, cols] = res.astype(BF16).reshape(nx, 2, nr, 256)
            s_core[s] = copy(y_buf.at[k, :, 1 - c, rs], sib_buf.at[k, :, rs], sib)

        def fold(s):
            k, r0, nr = subs[s]
            rs = pl.ds(r0, nr)
            s_core[s].wait_recv()
            s_x[s] = []
            for j in (2, 1, 3, 0):
                xb = (x + j) % nx
                y_buf[k, xb, c, rs] = (
                    y_buf[k, xb, c, rs].astype(F32) + sib_buf[k, xb, rs].astype(F32)).astype(BF16)
                if j:
                    s_x[s].append(copy(y_buf.at[k, xb, c, rs], q1.at[k, nx - j - 1, rs],
                                       x_peers[j - 1]))

        def settle(s):
            k, r0, nr = subs[s]
            rs = pl.ds(r0, nr)
            for d in s_x[s]:
                d.wait_recv()
            t_buf[k, rs] = (
                y_buf[k, x, c, rs].astype(F32) + q1[k, 0, rs].astype(F32)
                + q1[k, 1, rs].astype(F32) + q1[k, 2, rs].astype(F32)).astype(BF16)
            if k:
                s_z[s] = copy(t_buf.at[k, rs], zr.at[(nz - k) % nz - 1, rs], z_peers[k - 1])

        def z_take(p, i):
            xb, rs = rel[i], pl.ds(*parts[p])
            g_up[p, i].wait_recv()
            g_dn[p, i].wait_recv()
            k, dev = ((3, d_zp), (1, d_zm))[i % 2]
            forward[p].append(copy(x_buf.at[k, xb, c, rs], x_buf.at[2, xb, c, rs], dev))
            if i == 3:
                share(1, p)
                share(3, p)

        def z_last(p):
            for d in forward[p]:
                d.wait_recv()
            share(2, p)

        arrived, edges = set(), []

        def finish_rows(r0, nr):
            rs = pl.ds(r0, nr)
            for s, (k, first, count) in enumerate(subs):
                if k and first < r0 + nr and r0 < first + count and s not in arrived:
                    arrived.add(s)
                    s_z[s].wait_recv()
            ffn = t_buf[0, rs].astype(F32)
            for k in range(1, nz):
                ffn = ffn + zr[k - 1, rs].astype(F32)
            t_buf[0, rs] = ffn.astype(BF16)

        def send_edges():
            finish_rows(fixed, rows - fixed)
            edges.append(copy(t_buf.at[0, pl.ds(fixed, edge)], edge_next, d_prev))
            edges.append(copy(t_buf.at[0, pl.ds(rows - edge, edge)], edge_prev, d_next))

        forward = ([], [])
        z_take(0, 0)
        gate_up(0)
        settle_rows()
        z_take(0, 1)
        z_take(0, 2)
        z_take(0, 3)
        gate_up(1)
        take(1, 0)
        take(1, 1)
        gate_up(2)
        z_last(0)
        take(1, 2)
        gate_up(3)
        z_take(1, 0)
        combine(1)
        gate_up(4)
        activate(0)
        z_take(1, 1)
        z_take(1, 2)
        combine(3)
        z_take(1, 3)
        activate(1)
        gate_up(6)
        loads[2].wait()
        down(0)
        gate_up(7)
        pass_on(1)
        combine(6)
        z_last(1)
        combine(7)
        combine(2)
        fold(0)
        down(1)
        activate(6)
        gate_up(5)
        activate(7)
        pass_on(6)
        combine(5)
        pass_on(7)
        combine(4)
        fold(1)
        down(6)
        activate(2)
        fold(6)
        activate(5)
        down(7)
        settle(1)
        pass_on(2)
        activate(4)
        fold(7)
        pass_on(5)
        down(2)
        fold(2)
        down(5)
        pass_on(4)
        fold(5)
        settle(6)
        activate(3)
        down(4)
        pass_on(3)
        fold(4)
        settle(2)
        settle(7)
        settle(0)
        down(3)
        settle(5)
        fold(3)
        settle(4)
        send_edges()
        settle(3)

        finish_rows(0, fixed)
        span = rows + 2 * edge
        slot = lax.broadcasted_iota(jnp.int32, (most, span), 1).astype(F32)
        place = lax.broadcasted_iota(jnp.int32, (most, span), 0).astype(F32)
        aim = jnp.where(place < fixed, place, place + excess + fixed)
        shift = jnp.where(slot == aim, 1.0, 0.0).astype(F32).astype(BF16)
        pick = jnp.dot(match, shift, preferred_element_type=F32).astype(BF16)
        line = lax.broadcasted_iota(jnp.int32, (tok, tok), 0)
        col = lax.broadcasted_iota(jnp.int32, (tok, tok), 1)
        weight = jnp.sum(jnp.where(line == col, rw_ref[...], 0.0), axis=-1, keepdims=True)
        for d in edges:
            d.wait_recv()
        rows_all = jnp.concatenate(
            [t_buf[0, pl.ds(0, fixed)], edge_prev[...], t_buf[0, pl.ds(fixed, rows - fixed)],
             edge_next[...]], axis=0)
        added = jnp.dot(pick, rows_all, preferred_element_type=F32)
        out_ref[...] = (hid_ref[...].astype(F32) + weight * added).astype(BF16)

        for d in used:
            d.wait_send()

    vmem = pl.BlockSpec(memory_space=pltpu.VMEM)
    hbm = pl.BlockSpec(memory_space=pl.ANY)
    blocks = (nx, 2, rows, feat)
    return pl.pallas_call(
        kernel,
        out_shape=jax.ShapeDtypeStruct((tok, feat), BF16),
        in_specs=[pl.BlockSpec(memory_space=pltpu.SMEM), vmem, vmem, vmem, vmem, hbm, hbm, hbm],
        out_specs=vmem,
        scratch_shapes=[
            pltpu.VMEM((feat, 2 * units), BF16),
            pltpu.VMEM((units, feat), BF16),
            pltpu.VMEM((ny, 8, 128), F32),
            pltpu.VMEM((8, 8, 128), F32),
            pltpu.VMEM((nz, 8, 128), F32),
            pltpu.VMEM((edge, feat), BF16),
            pltpu.VMEM((edge, feat), BF16),
            pltpu.VMEM((edge, feat), BF16),
            pltpu.VMEM((edge, feat), BF16),
            pltpu.VMEM((nz,) + blocks, BF16),
            pltpu.VMEM((nz, ny, 2, rows, 2 * units), BF16),
            pltpu.VMEM((nz, 2, 2, rows, units), BF16),
            pltpu.VMEM((nz, 2, 2, 2, rows, units), BF16),
            pltpu.VMEM((nz, ny, 2, rows, units), BF16),
            pltpu.VMEM((nz,) + blocks, BF16),
            pltpu.VMEM((nz, nx, rows, feat), BF16),
            pltpu.VMEM((nz, nx - 1, rows, feat), BF16),
            pltpu.VMEM((nz, rows, feat), BF16),
            pltpu.VMEM((nz - 1, rows, feat), BF16),
            pltpu.VMEM((edge, feat), BF16),
            pltpu.VMEM((edge, feat), BF16),
            pltpu.SemaphoreType.DMA((3,)),
            pltpu.SemaphoreType.DMA((N_SEM,)),
            pltpu.SemaphoreType.DMA((N_SEM,)),
        ],
        compiler_params=pltpu.CompilerParams(
            collective_id=0, has_side_effects=True, vmem_limit_bytes=56 * 1024 * 1024),
    )(counts, selected, router_weight.reshape(1, tok), norm_gain.reshape(1, feat), hidden,
      w_gate, w_up, w_down)


def solution(mesh):
    n_ctx, n_tp = mesh.shape["ctx"], mesh.shape["tp"]
    placed = (
        P("ctx", "tp"),
        P("ctx"),
        P("ctx", None),
        P("ctx"),
        P("tp"),
        P("tp", "ctx"),
        P("tp", "ctx"),
        P("ctx", "tp"),
    )

    def step(*args):
        return body(*args, n_ctx, n_tp)

    return jax.shard_map(
        step, mesh=mesh, in_specs=placed, out_specs=P("ctx", "tp"), check_vma=False
    )
```

```python
import jax
import jax.numpy as jnp
from jax import lax
from jax.experimental import pallas as pl
from jax.experimental.pallas import tpu as pltpu
from jax.sharding import PartitionSpec as P

MESH = pl.DeviceIdType.MESH
F32 = jnp.float32
BF16 = jnp.bfloat16
N_SEM = 224


def body(hidden, counts, selected, router_weight, norm_gain, w_gate, w_up, w_down, n_ctx, n_tp):
    tok, feat = hidden.shape
    most = selected.shape[1]
    units = w_gate.shape[1]
    width = feat * n_tp
    rows = most * 2 // 3
    edge = 16
    nx, nz, ny = 4, n_ctx // 8, n_tp
    fixed = 16

    def kernel(cnt_hbm, sel_hbm, gain_hbm, hid_hbm, wg_hbm, wu_hbm, wd_hbm, out_ref,
               cnt_ref, sel_ref, gain_ref, hid_ref, w_gu, w_dn, sq, cnt, ztot, to_prev, to_next, from_next, from_prev,
               x_buf, part, r1, r2, h_buf, y_buf, sib_buf, q1, t_buf, zr,
               edge_next, edge_prev, load_sem, send_sem, recv_sem):
        ctx = lax.axis_index("ctx")
        y = lax.axis_index("tp")
        z, q = ctx // 8, ctx % 8
        x, c = q // 2, q % 2

        def at(zz, xx, cc):
            return (zz * nx + xx) * 2 + cc

        xp, xm, x2 = (x + 1) % nx, (x + nx - 1) % nx, (x + 2) % nx
        zp, zm = (z + 1) % nz, (z + nz - 1) % nz
        yp, ym, y2 = (y + 1) % ny, (y + ny - 1) % ny, (y + 2) % ny
        sib = (at(z, x, 1 - c), y)
        d_xp, d_xm = (at(z, xp, c), y), (at(z, xm, c), y)
        d_zp, d_zm = (at(zp, x, c), y), (at(zm, x, c), y)
        d_yp, d_ym = (ctx, yp), (ctx, ym)
        d_next, d_prev = ((ctx + 1) % n_ctx, y), ((ctx + n_ctx - 1) % n_ctx, y)

        loads = []
        for i, (src, dst) in enumerate((
            (hid_hbm, hid_ref),
            (cnt_hbm, cnt_ref),
            (sel_hbm, sel_ref),
            (gain_hbm, gain_ref),
            (wg_hbm, w_gu.at[:, pl.ds(0, units)]),
            (wu_hbm, w_gu.at[:, pl.ds(units, units)]),
            (wd_hbm, w_dn),
        )):
            load = pltpu.make_async_copy(src, dst, load_sem.at[i])
            load.start()
            loads.append(load)

        used = []

        def copy(src, dst, dev):
            i = len(used)
            d = pltpu.make_async_remote_copy(
                src_ref=src, dst_ref=dst, send_sem=send_sem.at[i], recv_sem=recv_sem.at[i],
                device_id=dev, device_id_type=MESH)
            used.append(d)
            d.start()
            return d

        row_peers = [(at(z, (q + j) % 8 // 2, (q + j) % 8 % 2), y) for j in range(1, 8)]
        x_peers = [(at(z, (x + j) % nx, c), y) for j in range(1, nx)]
        z_peers = [(at((z + j) % nz, x, c), y) for j in range(1, nz)]
        y_peers = [(ctx, (y + j) % ny) for j in range(1, ny)]

        barrier = pltpu.get_barrier_semaphore()
        peers = row_peers + z_peers + y_peers + [d_next, d_prev]
        for dev in peers:
            pl.semaphore_signal(barrier, inc=1, device_id=dev, device_id_type=MESH)

        for load in loads[:4]:
            load.wait()
        n_f = cnt_ref[...].astype(F32)
        cnt[q] = jnp.broadcast_to(n_f, (8, 128))
        hid = hid_ref[...].astype(F32)
        diagonal = (lax.broadcasted_iota(jnp.int32, (tok, 128), 0)
                    == lax.broadcasted_iota(jnp.int32, (tok, 128), 1))
        squares = jnp.sum(hid * hid, axis=-1, keepdims=True)
        sq[y] = jnp.broadcast_to(
            jnp.sum(jnp.where(diagonal, squares, 0.0), axis=0, keepdims=True), (8, 128))
        ids = lax.broadcasted_iota(jnp.int32, (tok, most), 0)
        rank = lax.broadcasted_iota(jnp.int32, (tok, most), 1).astype(F32)
        match = jnp.where((sel_ref[...] == ids) & (rank < n_f), 1.0, 0.0).astype(F32).astype(BF16)

        def chosen(count, offset, first, excess):
            slot = lax.broadcasted_iota(jnp.int32, (count, most), 0).astype(F32) + offset
            place = lax.broadcasted_iota(jnp.int32, (count, most), 1).astype(F32)
            here = (place < fixed) if first else (place >= fixed)
            shift = jnp.where((slot == place + excess) & here, 1.0, 0.0).astype(F32).astype(BF16)
            return lax.dot_general(
                shift, match, (((1,), (1,)), ((), ())), preferred_element_type=F32).astype(BF16)

        pick_fixed = chosen(fixed, 0, True, 0.0)
        raw = jnp.dot(pick_fixed, hid_ref[...], preferred_element_type=F32)

        pl.semaphore_wait(barrier, len(peers))

        c_sq = [copy(sq.at[y], sq.at[y], dev) for dev in y_peers]
        c_row = [copy(cnt.at[q], cnt.at[q], dev) for dev in row_peers]
        for d in c_sq:
            d.wait_recv()
        sums = sq[0]
        for j in range(1, ny):
            sums = sums + sq[j]
        scale_row = lax.rsqrt(sums / width + 1e-05)[0:1]
        scale_fixed = jnp.sum(
            pick_fixed.astype(F32) * scale_row[:, 0:tok], axis=-1, keepdims=True)
        x_buf[0, x, c, pl.ds(0, fixed)] = (raw * scale_fixed * gain_ref[...]).astype(BF16)

        parts = ((0, fixed), (fixed, rows - fixed))
        rel = [x, xm, xp, x2]
        g_x, g_up, g_dn, g_sib = {}, {}, {}, {}

        def spread(p, i):
            xb, rs = rel[i], pl.ds(*parts[p])
            g_up[p, i] = copy(x_buf.at[0, xb, c, rs], x_buf.at[3, xb, c, rs], d_zp)
            g_dn[p, i] = copy(x_buf.at[0, xb, c, rs], x_buf.at[1, xb, c, rs], d_zm)
            g_sib[0, p, i] = copy(x_buf.at[0, xb, c, rs], x_buf.at[0, xb, c, rs], sib)

        def share(k, p):
            rs = pl.ds(*parts[p])
            g_sib[k, p] = copy(x_buf.at[k, :, c, rs], x_buf.at[k, :, c, rs], sib)

        def offer(p):
            rs = pl.ds(*parts[p])
            g_x[p] = [copy(x_buf.at[0, x, c, rs], x_buf.at[0, x, c, rs], dev) for dev in x_peers]
            spread(p, 0)

        def take(p, n):
            i, j = ((1, 0), (2, 2), (3, 1))[n]
            g_x[p][j].wait_recv()
            spread(p, i)

        offer(0)
        scale = jnp.sum(jnp.where(diagonal, scale_row, 0.0), axis=-1, keepdims=True)
        normed = (hid_ref[...].astype(F32) * scale * gain_ref[...]).astype(BF16)

        for d in c_row:
            d.wait_recv()
        before = jnp.zeros((8, 128), F32)
        total = jnp.zeros((8, 128), F32)
        for j in range(8):
            before = before + cnt[j] * jnp.where(j < q, 1.0, 0.0).astype(F32)
            total = total + cnt[j]
        ztot[z] = total
        c_z = [copy(ztot.at[z], ztot.at[z], dev) for dev in z_peers]

        take(0, 0)
        take(0, 1)
        take(0, 2)
        loads[4].wait()
        loads[5].wait()
        for d in c_z:
            d.wait_recv()
        for j in range(nz):
            before = before + ztot[j] * jnp.where(j < z, 1.0, 0.0).astype(F32)
        excess = (before - (ctx * rows).astype(F32))[0:1, 0:1]
        to_prev[...] = jnp.dot(
            chosen(edge, 0, False, excess), normed, preferred_element_type=F32).astype(BF16)
        c_prev = copy(to_prev, from_next, d_prev)
        to_next[...] = jnp.dot(
            chosen(edge, rows, False, excess), normed, preferred_element_type=F32).astype(BF16)
        c_next = copy(to_next, from_prev, d_next)
        x_buf[0, x, c, pl.ds(fixed, rows - fixed)] = jnp.dot(
            chosen(rows - fixed, fixed, False, excess), normed, preferred_element_type=F32
        ).astype(BF16)

        def settle_rows():
            for d, got, r0 in ((c_next, from_prev, fixed), (c_prev, from_next, rows - edge)):
                d.wait_recv()
                x_buf[0, x, c, pl.ds(r0, edge)] = (
                    x_buf[0, x, c, pl.ds(r0, edge)].astype(F32) + got[...].astype(F32)
                ).astype(BF16)
            offer(1)

        subs = ((0, 0, 16), (1, 0, 16), (3, 0, 16), (2, 0, 16), (0, 16, 32), (2, 16, 32), (3, 16, 32), (1, 16, 32))
        direct = (0,)
        waited = set()
        gate, up = pl.ds(0, units), pl.ds(units, units)
        steps = (2 * units) // 256
        y_first, y_second, y_gather, y_pass = {}, {}, {}, {}

        def gate_up(s):
            k, r0, nr = subs[s]
            rs = pl.ds(r0, nr)
            for p, (first, count) in enumerate(parts):
                if first < r0 + nr and r0 < first + count and (k, p) not in waited:
                    waited.add((k, p))
                    for d in [g_sib[0, p, i] for i in range(4)] if k == 0 else [g_sib[k, p]]:
                        d.wait_recv()

            def column(j):
                cols = pl.ds(j * 256, 256)
                res = jnp.dot(x_buf[k, :, :, rs].reshape(nx * 2 * nr, feat), w_gu[:, cols],
                              preferred_element_type=F32)
                part[k, :, :, rs, cols] = res.astype(BF16).reshape(ny, 2, nr, 256)

            ready = -(-units // 256)
            sent = {}
            for kind, cols, tiles in ((0, gate, range(ready)), (1, up, range(ready, steps))):
                for j in tiles:
                    column(j)
                first, second = ((y2, d_yp), (y2, d_ym))[kind], ((ym, d_ym), (yp, d_yp))[kind]
                if s in direct:
                    sent[kind] = [copy(part.at[k, owner, :, rs, cols], place.at[:, rs], dev)
                                  for owner, dev, place in (
                                      (y2, (ctx, y2), r1.at[k, kind]),
                                      (yp, d_yp, r2.at[k, 0, kind]),
                                      (ym, d_ym, r2.at[k, 1, kind]))]
                else:
                    sent[kind] = (
                        copy(part.at[k, first[0], :, rs, cols], r1.at[k, kind, :, rs], first[1]),
                        copy(part.at[k, second[0], :, rs, cols], r2.at[k, 1 - kind, kind, :, rs],
                             second[1]))
            if s in direct:
                y_second[s] = sent[0] + sent[1]
            else:
                y_first[s] = (sent[0][0], sent[1][0])
                y_second[s] = [sent[0][1], sent[1][1]]

        def combine(s):
            k, r0, nr = subs[s]
            rs = pl.ds(r0, nr)
            y_first[s][0].wait_recv()
            part[k, yp, :, rs, gate] = (
                part[k, yp, :, rs, gate].astype(F32) + r1[k, 0, :, rs].astype(F32)).astype(BF16)
            y_second[s].append(copy(part.at[k, yp, :, rs, gate], r2.at[k, 0, 0, :, rs], d_yp))
            y_first[s][1].wait_recv()
            part[k, ym, :, rs, up] = (
                part[k, ym, :, rs, up].astype(F32) + r1[k, 1, :, rs].astype(F32)).astype(BF16)
            y_second[s].append(copy(part.at[k, ym, :, rs, up], r2.at[k, 1, 1, :, rs], d_ym))

        def activate(s):
            k, r0, nr = subs[s]
            rs = pl.ds(r0, nr)
            for d in y_second[s]:
                d.wait_recv()
            g = (part[k, y, :, rs, gate].astype(F32) + r2[k, 0, 0, :, rs].astype(F32)
                 + r2[k, 1, 0, :, rs].astype(F32))
            u = (part[k, y, :, rs, up].astype(F32) + r2[k, 0, 1, :, rs].astype(F32)
                 + r2[k, 1, 1, :, rs].astype(F32))
            if s in direct:
                g = g + r1[k, 0, :, rs].astype(F32)
                u = u + r1[k, 1, :, rs].astype(F32)
            h_buf[k, y, :, rs] = (g / (1.0 + jnp.exp(-g)) * u).astype(BF16)
            mine = h_buf.at[k, y, :, rs]
            y_gather[s] = (copy(mine, mine, d_yp), copy(mine, mine, d_ym))
            if s in direct:
                y_pass[s] = y_gather[s] + (copy(mine, mine, (ctx, y2)),)

        def pass_on(s):
            k, r0, nr = subs[s]
            rs = pl.ds(r0, nr)
            y_gather[s][0].wait_recv()
            left = h_buf.at[k, ym, 0, rs]
            f_p = copy(left, left, d_yp)
            y_gather[s][1].wait_recv()
            right = h_buf.at[k, yp, 1, rs]
            f_m = copy(right, right, d_ym)
            y_pass[s] = (f_p, f_m)

        s_core, s_x, s_z = {}, {}, {}

        def down(s):
            k, r0, nr = subs[s]
            rs = pl.ds(r0, nr)
            for d in y_pass[s]:
                d.wait_recv()

            for j in range(feat // 256):
                cols = pl.ds(j * 256, 256)
                res = jnp.dot(h_buf[k, :, :, rs].reshape(nx * 2 * nr, units), w_dn[:, cols],
                              preferred_element_type=F32)
                y_buf[k, :, :, rs, cols] = res.astype(BF16).reshape(nx, 2, nr, 256)
            s_core[s] = copy(y_buf.at[k, :, 1 - c, rs], sib_buf.at[k, :, rs], sib)

        def fold(s):
            k, r0, nr = subs[s]
            rs = pl.ds(r0, nr)
            s_core[s].wait_recv()
            s_x[s] = []
            for j in (2, 1, 3, 0):
                xb = (x + j) % nx
                y_buf[k, xb, c, rs] = (
                    y_buf[k, xb, c, rs].astype(F32) + sib_buf[k, xb, rs].astype(F32)).astype(BF16)
                if j:
                    s_x[s].append(copy(y_buf.at[k, xb, c, rs], q1.at[k, nx - j - 1, rs],
                                       x_peers[j - 1]))

        def settle(s):
            k, r0, nr = subs[s]
            rs = pl.ds(r0, nr)
            for d in s_x[s]:
                d.wait_recv()
            t_buf[k, rs] = (
                y_buf[k, x, c, rs].astype(F32) + q1[k, 0, rs].astype(F32)
                + q1[k, 1, rs].astype(F32) + q1[k, 2, rs].astype(F32)).astype(BF16)
            if k:
                s_z[s] = copy(t_buf.at[k, rs], zr.at[(nz - k) % nz - 1, rs], z_peers[k - 1])

        def z_take(p, i):
            xb, rs = rel[i], pl.ds(*parts[p])
            g_up[p, i].wait_recv()
            g_dn[p, i].wait_recv()
            k, dev = ((3, d_zp), (1, d_zm))[i % 2]
            forward[p].append(copy(x_buf.at[k, xb, c, rs], x_buf.at[2, xb, c, rs], dev))
            if i == 3:
                share(1, p)
                share(3, p)

        def z_last(p):
            for d in forward[p]:
                d.wait_recv()
            share(2, p)

        arrived, edges = set(), []

        def finish_rows(r0, nr):
            rs = pl.ds(r0, nr)
            for s, (k, first, count) in enumerate(subs):
                if k and first < r0 + nr and r0 < first + count and s not in arrived:
                    arrived.add(s)
                    s_z[s].wait_recv()
            ffn = t_buf[0, rs].astype(F32)
            for k in range(1, nz):
                ffn = ffn + zr[k - 1, rs].astype(F32)
            t_buf[0, rs] = ffn.astype(BF16)

        def send_edges():
            finish_rows(fixed, rows - fixed)
            edges.append(copy(t_buf.at[0, pl.ds(fixed, edge)], edge_next, d_prev))
            edges.append(copy(t_buf.at[0, pl.ds(rows - edge, edge)], edge_prev, d_next))

        forward = ([], [])
        settle_rows()
        z_take(0, 0)
        gate_up(0)
        z_take(0, 1)
        z_take(0, 2)
        z_take(0, 3)
        gate_up(1)
        take(1, 0)
        take(1, 1)
        take(1, 2)
        activate(0)
        gate_up(4)
        z_last(0)
        loads[6].wait()
        down(0)
        gate_up(3)
        z_take(1, 0)
        combine(4)
        z_take(1, 1)
        z_take(1, 2)
        z_take(1, 3)
        gate_up(7)
        gate_up(6)
        activate(4)
        combine(6)
        z_last(1)
        combine(7)
        pass_on(4)
        activate(6)
        gate_up(5)
        down(4)
        pass_on(6)
        combine(5)
        fold(4)
        activate(7)
        fold(0)
        activate(5)
        down(6)
        pass_on(7)
        gate_up(2)
        fold(6)
        combine(3)
        pass_on(5)
        down(7)
        combine(1)
        fold(7)
        activate(3)
        combine(2)
        down(5)
        activate(1)
        pass_on(3)
        settle(0)
        fold(5)
        activate(2)
        down(3)
        pass_on(1)
        pass_on(2)
        settle(6)
        fold(3)
        settle(7)
        down(1)
        fold(1)
        settle(5)
        down(2)
        settle(4)
        fold(2)
        settle(3)
        send_edges()
        settle(1)
        settle(2)

        span = rows + 2 * edge
        slot = lax.broadcasted_iota(jnp.int32, (most, span), 1).astype(F32)
        place = lax.broadcasted_iota(jnp.int32, (most, span), 0).astype(F32)
        aim = jnp.where(place < fixed, place, place + excess + fixed)
        shift = jnp.where(slot == aim, 1.0, 0.0).astype(F32).astype(BF16)
        pick = jnp.dot(match, shift, preferred_element_type=F32).astype(BF16)
        for d in edges:
            d.wait_recv()
        others = jnp.concatenate(
            [edge_prev[...], t_buf[0, pl.ds(fixed, rows - fixed)], edge_next[...]], axis=0)
        base = jnp.dot(pick[:, fixed:], others, preferred_element_type=F32)
        finish_rows(0, fixed)
        added = base + jnp.dot(
            pick[:, 0:fixed], t_buf[0, pl.ds(0, fixed)], preferred_element_type=F32)
        out_ref[...] = added.astype(BF16)

        for d in used:
            d.wait_send()

    vmem = pl.BlockSpec(memory_space=pltpu.VMEM)
    hbm = pl.BlockSpec(memory_space=pl.ANY)
    blocks = (nx, 2, rows, feat)
    added = pl.pallas_call(
        kernel,
        out_shape=jax.ShapeDtypeStruct((tok, feat), BF16),
        in_specs=[hbm] * 7,
        out_specs=vmem,
        scratch_shapes=[
            pltpu.VMEM((1, 1), jnp.int32),
            pltpu.VMEM((1, most), jnp.int32),
            pltpu.VMEM((1, feat), F32),
            pltpu.VMEM((tok, feat), BF16),
            pltpu.VMEM((feat, 2 * units), BF16),
            pltpu.VMEM((units, feat), BF16),
            pltpu.VMEM((ny, 8, 128), F32),
            pltpu.VMEM((8, 8, 128), F32),
            pltpu.VMEM((nz, 8, 128), F32),
            pltpu.VMEM((edge, feat), BF16),
            pltpu.VMEM((edge, feat), BF16),
            pltpu.VMEM((edge, feat), BF16),
            pltpu.VMEM((edge, feat), BF16),
            pltpu.VMEM((nz,) + blocks, BF16),
            pltpu.VMEM((nz, ny, 2, rows, 2 * units), BF16),
            pltpu.VMEM((nz, 2, 2, rows, units), BF16),
            pltpu.VMEM((nz, 2, 2, 2, rows, units), BF16),
            pltpu.VMEM((nz, ny, 2, rows, units), BF16),
            pltpu.VMEM((nz,) + blocks, BF16),
            pltpu.VMEM((nz, nx, rows, feat), BF16),
            pltpu.VMEM((nz, nx - 1, rows, feat), BF16),
            pltpu.VMEM((nz, rows, feat), BF16),
            pltpu.VMEM((nz - 1, rows, feat), BF16),
            pltpu.VMEM((edge, feat), BF16),
            pltpu.VMEM((edge, feat), BF16),
            pltpu.SemaphoreType.DMA((7,)),
            pltpu.SemaphoreType.DMA((N_SEM,)),
            pltpu.SemaphoreType.DMA((N_SEM,)),
        ],
        compiler_params=pltpu.CompilerParams(
            collective_id=0, has_side_effects=True, vmem_limit_bytes=56 * 1024 * 1024),
    )(counts.reshape(1, 1), selected, norm_gain.reshape(1, feat), hidden, w_gate, w_up, w_down)
    return (hidden.astype(F32) + router_weight[:, None] * added.astype(F32)).astype(BF16)


def solution(mesh):
    n_ctx, n_tp = mesh.shape["ctx"], mesh.shape["tp"]
    placed = (
        P("ctx", "tp"),
        P("ctx"),
        P("ctx", None),
        P("ctx"),
        P("tp"),
        P("tp", "ctx"),
        P("tp", "ctx"),
        P("ctx", "tp"),
    )

    def step(*args):
        return body(*args, n_ctx, n_tp)

    return jax.shard_map(
        step, mesh=mesh, in_specs=placed, out_specs=P("ctx", "tp"), check_vma=False
    )
```

```python
import jax
import jax.numpy as jnp
from jax import lax
from jax.experimental import pallas as pl
from jax.experimental.pallas import tpu as pltpu
from jax.sharding import PartitionSpec as P

MESH = pl.DeviceIdType.MESH
F32 = jnp.float32
BF16 = jnp.bfloat16
N_SEM = 224


def body(hidden, counts, selected, router_weight, norm_gain, w_gate, w_up, w_down, n_ctx, n_tp):
    tok, feat = hidden.shape
    most = selected.shape[1]
    units = w_gate.shape[1]
    width = feat * n_tp
    rows = most * 2 // 3
    edge = 16
    nx, nz, ny = 4, n_ctx // 8, n_tp
    fixed = 16

    def kernel(cnt_hbm, sel_hbm, gain_hbm, hid_hbm, wg_hbm, wu_hbm, wd_hbm, out_ref,
               cnt_ref, sel_ref, gain_ref, hid_ref, w_gu, w_dn, sq, cnt, ztot, to_prev, to_next, from_next, from_prev,
               x_buf, part, r1, r2, h_buf, y_buf, sib_buf, q1, t_buf, zr,
               edge_next, edge_prev, load_sem, send_sem, recv_sem):
        ctx = lax.axis_index("ctx")
        y = lax.axis_index("tp")
        z, q = ctx // 8, ctx % 8
        x, c = q // 2, q % 2

        def at(zz, xx, cc):
            return (zz * nx + xx) * 2 + cc

        xp, xm, x2 = (x + 1) % nx, (x + nx - 1) % nx, (x + 2) % nx
        zp, zm = (z + 1) % nz, (z + nz - 1) % nz
        yp, ym, y2 = (y + 1) % ny, (y + ny - 1) % ny, (y + 2) % ny
        sib = (at(z, x, 1 - c), y)
        d_xp, d_xm = (at(z, xp, c), y), (at(z, xm, c), y)
        d_zp, d_zm = (at(zp, x, c), y), (at(zm, x, c), y)
        d_yp, d_ym = (ctx, yp), (ctx, ym)
        d_next, d_prev = ((ctx + 1) % n_ctx, y), ((ctx + n_ctx - 1) % n_ctx, y)

        used = []

        def copy(src, dst, dev):
            i = len(used)
            d = pltpu.make_async_remote_copy(
                src_ref=src, dst_ref=dst, send_sem=send_sem.at[i], recv_sem=recv_sem.at[i],
                device_id=dev, device_id_type=MESH)
            used.append(d)
            d.start()
            return d

        row_peers = [(at(z, (q + j) % 8 // 2, (q + j) % 8 % 2), y) for j in range(1, 8)]
        x_peers = [(at(z, (x + j) % nx, c), y) for j in range(1, nx)]
        z_peers = [(at((z + j) % nz, x, c), y) for j in range(1, nz)]
        y_peers = [(ctx, (y + j) % ny) for j in range(1, ny)]

        barrier = pltpu.get_barrier_semaphore()
        peers = row_peers + z_peers + y_peers + [d_next, d_prev]
        for dev in peers:
            pl.semaphore_signal(barrier, inc=1, device_id=dev, device_id_type=MESH)

        loads = []
        for i, (src, dst) in enumerate((
            (hid_hbm, hid_ref),
            (cnt_hbm, cnt_ref),
            (sel_hbm, sel_ref),
            (gain_hbm, gain_ref),
            (wg_hbm, w_gu.at[:, pl.ds(0, units)]),
            (wu_hbm, w_gu.at[:, pl.ds(units, units)]),
            (wd_hbm, w_dn),
        )):
            load = pltpu.make_async_copy(src, dst, load_sem.at[i])
            load.start()
            loads.append(load)

        for load in loads[:4]:
            load.wait()
        n_f = cnt_ref[...].astype(F32)
        cnt[q] = jnp.broadcast_to(n_f, (8, 128))
        hid = hid_ref[...].astype(F32)
        diagonal = (lax.broadcasted_iota(jnp.int32, (tok, 128), 0)
                    == lax.broadcasted_iota(jnp.int32, (tok, 128), 1))
        squares = jnp.sum(hid * hid, axis=-1, keepdims=True)
        sq[y] = jnp.broadcast_to(
            jnp.sum(jnp.where(diagonal, squares, 0.0), axis=0, keepdims=True), (8, 128))
        pl.semaphore_wait(barrier, len(peers))

        c_sq = [copy(sq.at[y], sq.at[y], dev) for dev in y_peers]
        c_row = [copy(cnt.at[q], cnt.at[q], dev) for dev in row_peers]
        ids = lax.broadcasted_iota(jnp.int32, (tok, most), 0)
        rank = lax.broadcasted_iota(jnp.int32, (tok, most), 1).astype(F32)
        match = jnp.where((sel_ref[...] == ids) & (rank < n_f), 1.0, 0.0).astype(F32).astype(BF16)

        def chosen(count, offset, first, excess):
            slot = lax.broadcasted_iota(jnp.int32, (count, most), 0).astype(F32) + offset
            place = lax.broadcasted_iota(jnp.int32, (count, most), 1).astype(F32)
            here = (place < fixed) if first else (place >= fixed)
            shift = jnp.where((slot == place + excess) & here, 1.0, 0.0).astype(F32).astype(BF16)
            return lax.dot_general(
                shift, match, (((1,), (1,)), ((), ())), preferred_element_type=F32).astype(BF16)

        pick_fixed = chosen(fixed, 0, True, 0.0)
        raw = jnp.dot(pick_fixed, hid_ref[...], preferred_element_type=F32)
        for d in c_sq:
            d.wait_recv()
        sums = sq[0]
        for j in range(1, ny):
            sums = sums + sq[j]
        scale_row = lax.rsqrt(sums / width + 1e-05)[0:1]
        scale_fixed = jnp.sum(
            pick_fixed.astype(F32) * scale_row[:, 0:tok], axis=-1, keepdims=True)
        x_buf[0, x, c, pl.ds(0, fixed)] = (raw * scale_fixed * gain_ref[...]).astype(BF16)

        parts = ((0, fixed), (fixed, rows - fixed))
        rel = [x, xm, xp, x2]
        g_x, g_up, g_dn, g_sib = {}, {}, {}, {}

        def spread(p, i):
            xb, rs = rel[i], pl.ds(*parts[p])
            g_up[p, i] = copy(x_buf.at[0, xb, c, rs], x_buf.at[3, xb, c, rs], d_zp)
            g_dn[p, i] = copy(x_buf.at[0, xb, c, rs], x_buf.at[1, xb, c, rs], d_zm)
            g_sib[0, p, i] = copy(x_buf.at[0, xb, c, rs], x_buf.at[0, xb, c, rs], sib)

        def share(k, p):
            rs = pl.ds(*parts[p])
            g_sib[k, p] = copy(x_buf.at[k, :, c, rs], x_buf.at[k, :, c, rs], sib)

        def offer(p):
            rs = pl.ds(*parts[p])
            far, near_p, near_m = (
                copy(x_buf.at[0, x, c, rs], x_buf.at[0, x, c, rs], x_peers[j]) for j in (1, 0, 2))
            g_x[p] = [near_p, far, near_m]
            spread(p, 0)

        def take(p, n):
            i, j = ((1, 0), (2, 2), (3, 1))[n]
            g_x[p][j].wait_recv()
            spread(p, i)

        offer(0)
        scale = jnp.sum(jnp.where(diagonal, scale_row, 0.0), axis=-1, keepdims=True)
        normed = (hid_ref[...].astype(F32) * scale * gain_ref[...]).astype(BF16)

        for d in c_row:
            d.wait_recv()
        before = jnp.zeros((8, 128), F32)
        total = jnp.zeros((8, 128), F32)
        for j in range(8):
            before = before + cnt[j] * jnp.where(j < q, 1.0, 0.0).astype(F32)
            total = total + cnt[j]
        ztot[z] = total
        c_z = [copy(ztot.at[z], ztot.at[z], dev) for dev in z_peers]

        take(0, 0)
        take(0, 1)
        take(0, 2)
        loads[4].wait()
        loads[5].wait()
        for d in c_z:
            d.wait_recv()
        for j in range(nz):
            before = before + ztot[j] * jnp.where(j < z, 1.0, 0.0).astype(F32)
        excess = (before - (ctx * rows).astype(F32))[0:1, 0:1]
        to_prev[...] = jnp.dot(
            chosen(edge, 0, False, excess), normed, preferred_element_type=F32).astype(BF16)
        c_prev = copy(to_prev, from_next, d_prev)
        to_next[...] = jnp.dot(
            chosen(edge, rows, False, excess), normed, preferred_element_type=F32).astype(BF16)
        c_next = copy(to_next, from_prev, d_next)
        x_buf[0, x, c, pl.ds(fixed, rows - fixed)] = jnp.dot(
            chosen(rows - fixed, fixed, False, excess), normed, preferred_element_type=F32
        ).astype(BF16)

        def settle_rows():
            for d, got, r0 in ((c_next, from_prev, fixed), (c_prev, from_next, rows - edge)):
                d.wait_recv()
                x_buf[0, x, c, pl.ds(r0, edge)] = (
                    x_buf[0, x, c, pl.ds(r0, edge)].astype(F32) + got[...].astype(F32)
                ).astype(BF16)
            offer(1)

        subs = ((0, 0, 16), (1, 0, 16), (3, 0, 16), (2, 0, 16), (0, 16, 32), (2, 16, 32), (3, 16, 32), (1, 16, 32))
        direct = (0,)
        fine = ()
        waited = set()

        def spans(s):
            n = 2 if s in fine else 1
            return [pl.ds(i * (feat // n), feat // n) for i in range(n)]

        gate, up = pl.ds(0, units), pl.ds(units, units)
        steps = (2 * units) // 256
        y_first, y_second, y_gather, y_pass = {}, {}, {}, {}

        def gate_up(s):
            k, r0, nr = subs[s]
            rs = pl.ds(r0, nr)
            for p, (first, count) in enumerate(parts):
                if first < r0 + nr and r0 < first + count and (k, p) not in waited:
                    waited.add((k, p))
                    for d in [g_sib[0, p, i] for i in range(4)] if k == 0 else [g_sib[k, p]]:
                        d.wait_recv()

            def column(j):
                cols = pl.ds(j * 256, 256)
                res = jnp.dot(x_buf[k, :, :, rs].reshape(nx * 2 * nr, feat), w_gu[:, cols],
                              preferred_element_type=F32)
                part[k, :, :, rs, cols] = res.astype(BF16).reshape(ny, 2, nr, 256)

            ready = -(-units // 256)
            sent = {}
            for kind, cols, tiles in ((0, gate, range(ready)), (1, up, range(ready, steps))):
                for j in tiles:
                    column(j)
                first, second = ((y2, d_yp), (y2, d_ym))[kind], ((ym, d_ym), (yp, d_yp))[kind]
                if s in direct:
                    sent[kind] = [copy(part.at[k, owner, :, rs, cols], place.at[:, rs], dev)
                                  for owner, dev, place in (
                                      (y2, (ctx, y2), r1.at[k, kind]),
                                      (yp, d_yp, r2.at[k, 0, kind]),
                                      (ym, d_ym, r2.at[k, 1, kind]))]
                else:
                    sent[kind] = (
                        copy(part.at[k, first[0], :, rs, cols], r1.at[k, kind, :, rs], first[1]),
                        copy(part.at[k, second[0], :, rs, cols], r2.at[k, 1 - kind, kind, :, rs],
                             second[1]))
            if s in direct:
                y_second[s] = sent[0] + sent[1]
            else:
                y_first[s] = (sent[0][0], sent[1][0])
                y_second[s] = [sent[0][1], sent[1][1]]

        def combine(s):
            k, r0, nr = subs[s]
            rs = pl.ds(r0, nr)
            y_first[s][0].wait_recv()
            part[k, yp, :, rs, gate] = (
                part[k, yp, :, rs, gate].astype(F32) + r1[k, 0, :, rs].astype(F32)).astype(BF16)
            y_second[s].append(copy(part.at[k, yp, :, rs, gate], r2.at[k, 0, 0, :, rs], d_yp))
            y_first[s][1].wait_recv()
            part[k, ym, :, rs, up] = (
                part[k, ym, :, rs, up].astype(F32) + r1[k, 1, :, rs].astype(F32)).astype(BF16)
            y_second[s].append(copy(part.at[k, ym, :, rs, up], r2.at[k, 1, 1, :, rs], d_ym))

        def activate(s):
            k, r0, nr = subs[s]
            rs = pl.ds(r0, nr)
            for d in y_second[s]:
                d.wait_recv()
            g = (part[k, y, :, rs, gate].astype(F32) + r2[k, 0, 0, :, rs].astype(F32)
                 + r2[k, 1, 0, :, rs].astype(F32))
            u = (part[k, y, :, rs, up].astype(F32) + r2[k, 0, 1, :, rs].astype(F32)
                 + r2[k, 1, 1, :, rs].astype(F32))
            if s in direct:
                g = g + r1[k, 0, :, rs].astype(F32)
                u = u + r1[k, 1, :, rs].astype(F32)
            h_buf[k, y, :, rs] = (g / (1.0 + jnp.exp(-g)) * u).astype(BF16)
            mine = h_buf.at[k, y, :, rs]
            y_gather[s] = (copy(mine, mine, d_yp), copy(mine, mine, d_ym))
            if s in direct:
                y_pass[s] = y_gather[s] + (copy(mine, mine, (ctx, y2)),)

        def pass_on(s):
            k, r0, nr = subs[s]
            rs = pl.ds(r0, nr)
            y_gather[s][0].wait_recv()
            left = h_buf.at[k, ym, 0, rs]
            f_p = copy(left, left, d_yp)
            y_gather[s][1].wait_recv()
            right = h_buf.at[k, yp, 1, rs]
            f_m = copy(right, right, d_ym)
            y_pass[s] = (f_p, f_m)

        s_core, s_x, s_z = {}, {}, {}

        def down(s):
            k, r0, nr = subs[s]
            rs = pl.ds(r0, nr)
            for d in y_pass[s]:
                d.wait_recv()

            s_core[s] = []
            for cut in spans(s):
                for j in range(cut.start // 256, (cut.start + cut.size) // 256):
                    cols = pl.ds(j * 256, 256)
                    res = jnp.dot(h_buf[k, :, :, rs].reshape(nx * 2 * nr, units), w_dn[:, cols],
                                  preferred_element_type=F32)
                    y_buf[k, :, :, rs, cols] = res.astype(BF16).reshape(nx, 2, nr, 256)
                s_core[s].append(
                    copy(y_buf.at[k, :, 1 - c, rs, cut], sib_buf.at[k, :, rs, cut], sib))

        def fold(s):
            k, r0, nr = subs[s]
            rs = pl.ds(r0, nr)
            s_x[s] = []
            for cut, arriving in zip(spans(s), s_core[s]):
                arriving.wait_recv()
                sent = []
                for j in (2, 1, 3, 0):
                    xb = (x + j) % nx
                    y_buf[k, xb, c, rs, cut] = (
                        y_buf[k, xb, c, rs, cut].astype(F32)
                        + sib_buf[k, xb, rs, cut].astype(F32)).astype(BF16)
                    if j:
                        sent.append(copy(y_buf.at[k, xb, c, rs, cut],
                                         q1.at[k, nx - j - 1, rs, cut], x_peers[j - 1]))
                s_x[s].append(sent)

        def settle(s):
            k, r0, nr = subs[s]
            rs = pl.ds(r0, nr)
            s_z[s] = []
            for cut, sent in zip(spans(s), s_x[s]):
                for d in sent:
                    d.wait_recv()
                t_buf[k, rs, cut] = (
                    y_buf[k, x, c, rs, cut].astype(F32) + q1[k, 0, rs, cut].astype(F32)
                    + q1[k, 1, rs, cut].astype(F32) + q1[k, 2, rs, cut].astype(F32)).astype(BF16)
                if k:
                    s_z[s].append(copy(t_buf.at[k, rs, cut], zr.at[(nz - k) % nz - 1, rs, cut],
                                       z_peers[k - 1]))

        def z_take(p, i):
            xb, rs = rel[i], pl.ds(*parts[p])
            g_up[p, i].wait_recv()
            g_dn[p, i].wait_recv()
            k, dev = ((3, d_zp), (1, d_zm))[i % 2]
            forward[p].append(copy(x_buf.at[k, xb, c, rs], x_buf.at[2, xb, c, rs], dev))
            if i == 3:
                share(1, p)
                share(3, p)

        def z_last(p):
            for d in forward[p]:
                d.wait_recv()
            share(2, p)

        arrived, edges = set(), []

        def finish_rows(r0, nr):
            rs = pl.ds(r0, nr)
            for s, (k, first, count) in enumerate(subs):
                if k and first < r0 + nr and r0 < first + count and s not in arrived:
                    arrived.add(s)
                    for d in s_z[s]:
                        d.wait_recv()
            ffn = t_buf[0, rs].astype(F32)
            for k in range(1, nz):
                ffn = ffn + zr[k - 1, rs].astype(F32)
            t_buf[0, rs] = ffn.astype(BF16)

        def send_edges():
            finish_rows(fixed, rows - fixed)
            edges.append(copy(t_buf.at[0, pl.ds(fixed, edge)], edge_next, d_prev))
            edges.append(copy(t_buf.at[0, pl.ds(rows - edge, edge)], edge_prev, d_next))

        forward = ([], [])
        settle_rows()
        z_take(0, 0)
        gate_up(0)
        z_take(0, 1)
        z_take(0, 2)
        z_take(0, 3)
        gate_up(1)
        take(1, 0)
        take(1, 1)
        take(1, 2)
        activate(0)
        gate_up(4)
        z_last(0)
        loads[6].wait()
        down(0)
        gate_up(3)
        z_take(1, 0)
        combine(4)
        z_take(1, 1)
        z_take(1, 2)
        z_take(1, 3)
        gate_up(7)
        gate_up(6)
        activate(4)
        combine(6)
        z_last(1)
        combine(7)
        pass_on(4)
        activate(6)
        gate_up(5)
        down(4)
        pass_on(6)
        combine(5)
        fold(4)
        activate(7)
        fold(0)
        activate(5)
        down(6)
        pass_on(7)
        gate_up(2)
        fold(6)
        combine(3)
        pass_on(5)
        down(7)
        combine(1)
        fold(7)
        activate(3)
        combine(2)
        down(5)
        activate(1)
        pass_on(3)
        settle(0)
        fold(5)
        activate(2)
        down(3)
        pass_on(1)
        pass_on(2)
        settle(6)
        fold(3)
        settle(7)
        down(1)
        fold(1)
        settle(5)
        down(2)
        settle(4)
        fold(2)
        settle(3)
        send_edges()
        settle(1)
        settle(2)

        span = rows + 2 * edge
        slot = lax.broadcasted_iota(jnp.int32, (most, span), 1).astype(F32)
        place = lax.broadcasted_iota(jnp.int32, (most, span), 0).astype(F32)
        aim = jnp.where(place < fixed, place, place + excess + fixed)
        shift = jnp.where(slot == aim, 1.0, 0.0).astype(F32).astype(BF16)
        pick = jnp.dot(match, shift, preferred_element_type=F32).astype(BF16)
        for d in edges:
            d.wait_recv()
        others = jnp.concatenate(
            [edge_prev[...], t_buf[0, pl.ds(fixed, rows - fixed)], edge_next[...]], axis=0)
        base = jnp.dot(pick[:, fixed:], others, preferred_element_type=F32)
        finish_rows(0, fixed)
        added = base + jnp.dot(
            pick[:, 0:fixed], t_buf[0, pl.ds(0, fixed)], preferred_element_type=F32)
        out_ref[...] = added.astype(BF16)

        for d in used:
            d.wait_send()

    vmem = pl.BlockSpec(memory_space=pltpu.VMEM)
    hbm = pl.BlockSpec(memory_space=pl.ANY)
    blocks = (nx, 2, rows, feat)
    added = pl.pallas_call(
        kernel,
        out_shape=jax.ShapeDtypeStruct((tok, feat), BF16),
        in_specs=[hbm] * 7,
        out_specs=vmem,
        scratch_shapes=[
            pltpu.VMEM((1, 1), jnp.int32),
            pltpu.VMEM((1, most), jnp.int32),
            pltpu.VMEM((1, feat), F32),
            pltpu.VMEM((tok, feat), BF16),
            pltpu.VMEM((feat, 2 * units), BF16),
            pltpu.VMEM((units, feat), BF16),
            pltpu.VMEM((ny, 8, 128), F32),
            pltpu.VMEM((8, 8, 128), F32),
            pltpu.VMEM((nz, 8, 128), F32),
            pltpu.VMEM((edge, feat), BF16),
            pltpu.VMEM((edge, feat), BF16),
            pltpu.VMEM((edge, feat), BF16),
            pltpu.VMEM((edge, feat), BF16),
            pltpu.VMEM((nz,) + blocks, BF16),
            pltpu.VMEM((nz, ny, 2, rows, 2 * units), BF16),
            pltpu.VMEM((nz, 2, 2, rows, units), BF16),
            pltpu.VMEM((nz, 2, 2, 2, rows, units), BF16),
            pltpu.VMEM((nz, ny, 2, rows, units), BF16),
            pltpu.VMEM((nz,) + blocks, BF16),
            pltpu.VMEM((nz, nx, rows, feat), BF16),
            pltpu.VMEM((nz, nx - 1, rows, feat), BF16),
            pltpu.VMEM((nz, rows, feat), BF16),
            pltpu.VMEM((nz - 1, rows, feat), BF16),
            pltpu.VMEM((edge, feat), BF16),
            pltpu.VMEM((edge, feat), BF16),
            pltpu.SemaphoreType.DMA((7,)),
            pltpu.SemaphoreType.DMA((N_SEM,)),
            pltpu.SemaphoreType.DMA((N_SEM,)),
        ],
        compiler_params=pltpu.CompilerParams(
            collective_id=0, has_side_effects=True, vmem_limit_bytes=56 * 1024 * 1024),
    )(counts.reshape(1, 1), selected, norm_gain.reshape(1, feat), hidden, w_gate, w_up, w_down)
    return (hidden.astype(F32) + router_weight[:, None] * added.astype(F32)).astype(BF16)


def solution(mesh):
    n_ctx, n_tp = mesh.shape["ctx"], mesh.shape["tp"]
    placed = (
        P("ctx", "tp"),
        P("ctx"),
        P("ctx", None),
        P("ctx"),
        P("tp"),
        P("tp", "ctx"),
        P("tp", "ctx"),
        P("ctx", "tp"),
    )

    def step(*args):
        return body(*args, n_ctx, n_tp)

    return jax.shard_map(
        step, mesh=mesh, in_specs=placed, out_specs=P("ctx", "tp"), check_vma=False
    )
```
